32 devices in a mesh: row: 4 (over z), col: 8 (over y, x, core).
Axes of the slice: x: 2, y: 2, z: 4, core: 2. Of those that a mesh axis runs over, the one named last changes fastest.
Arguments:
- state_start: bfloat16 [512, 2048], P('row', 'col'), may hold values from -360 to 360
- actions: int32 [512, 2], P('row'), may hold values from 0 to 17
- targets: bfloat16 [2, 512, 2048], P(None, 'row'), may hold values from -504 to 504
- w_in: bfloat16 [2048, 4096], P('row', 'col'), may hold values from -0.125 to 0.125
- w_out: bfloat16 [4096, 2048], P('col', 'row'), may hold values from -0.09375 to 0.09375
- action_embed: bfloat16 [18, 4096], P(None, 'col'), may hold values from -6 to 6
Outputs:
- grad_w_in: float32 [2048, 4096], P('row', 'col')
- grad_w_out: float32 [4096, 2048], P('col', 'row')
The draws below stay inside these ranges and needn't reach their ends.
All inputs are finite; a program needn't handle non-finite values.
Results may differ from the reference program's by a relative error of at most 0.035.
Values may be sent and summed in bfloat16 or wider, within the bound.
A program may use at most 64 MiB of HBM per device.

```python
import math
import jax
import jax.numpy as jnp
from jax import lax

D = 2048
FF = 4096
ACTIONS = 18
UNROLL = 2
ROWS = 512
N_COL = 8


def joint_fields(key):
    row_key = jax.random.fold_in(key, 11)
    base_key = jax.random.fold_in(key, 12)
    noise_key = jax.random.fold_in(key, 13)
    row_scale = jnp.exp(jax.random.uniform(row_key, (ROWS, 1), jnp.float32, 0.0, math.log(10.0)))
    feature = jnp.arange(D, dtype=jnp.float32) / D
    col_scale = jnp.exp(math.log(3.0) * feature)[None, :]
    base = jnp.clip(jax.random.normal(base_key, (ROWS, D), jnp.float32), -4.0, 4.0)
    noise = jnp.clip(jax.random.normal(noise_key, (UNROLL, ROWS, D), jnp.float32), -4.0, 4.0)
    start = base * row_scale * col_scale
    target_field = 0.6 * start[None] + 0.8 * noise * row_scale[None] * col_scale[None]
    return (start, target_field)


def draw_state_start(key, part):
    start, target_field = joint_fields(key)
    return start.astype(jnp.bfloat16)


def draw_targets(key, part):
    start, target_field = joint_fields(key)
    return target_field.astype(jnp.bfloat16)


def touch_ends(entries, own_key, smallest, largest):
    longest = entries.shape.index(max(entries.shape))
    spots = []
    for shift in (0, 1):
        where = [jax.random.randint(jax.random.fold_in(own_key, axis), (), 0, length) for axis, length in enumerate(entries.shape)]
        where[longest] = (where[longest] + shift) % entries.shape[longest]
        spots.append(tuple(where))
    return entries.at[spots[0]].set(smallest).at[spots[1]].set(largest)


def level_of(rng, shape, split, smallest, largest):
    gain = 1.0
    for axis_at, shards_of in split:
        heights = jax.random.uniform(jax.random.fold_in(jax.random.fold_in(rng, 6), axis_at), (shards_of,), jnp.float32, smallest / len(split), largest / len(split))
        gain = gain * jnp.repeat(jnp.exp(heights), shape[axis_at] // shards_of).reshape((-1,) + (1,) * (len(shape) - 1 - axis_at))
    return gain


def centred(own_key, extent, width, reach, cuts=(), held_as=jnp.bfloat16):
    entries = width * jax.random.normal(own_key, extent, jnp.float32)
    if cuts:
        entries = entries * level_of(own_key, extent, cuts, -0.22, 0.18)
    return jnp.clip(entries, -reach, reach).astype(held_as)


def setup_inputs(seed: int = 0) -> dict:
    splits = jax.random.split(jax.random.key(seed), 7)
    state_start = draw_state_start(jax.random.fold_in(splits[6], 71), 0)
    actions = touch_ends(jax.random.randint(splits[1], (ROWS, UNROLL), 0, ACTIONS), jax.random.fold_in(splits[1], 1), 0, ACTIONS - 1).astype(jnp.int32)
    targets = draw_targets(jax.random.fold_in(splits[6], 71), 0)
    w_in = centred(splits[3], (D, FF), D ** -0.5, 0.125, ((0, 4), (1, 8)))
    w_out = centred(splits[4], (FF, D), FF ** -0.5, 0.09375, ((0, 8), (1, 4)))
    action_embed = centred(splits[5], (ACTIONS, FF), 1.0, 6.0, ((1, 8),))
    return dict(state_start=state_start, actions=actions, targets=targets, w_in=w_in, w_out=w_out, action_embed=action_embed)


EPS = 1e-06
LOSS_SCALE = 128.0

def silu_grad(pre_act):
    gate_val = jax.nn.sigmoid(pre_act)
    return gate_val * (1.0 + pre_act * (1.0 - gate_val))

def cosine_grad(state, target):
    state_f = state.astype(jnp.float32)
    target_f = target.astype(jnp.float32)
    self_dot = lax.optimization_barrier(jnp.sum(state_f * state_f, axis=-1, keepdims=True))
    cross_dot = lax.optimization_barrier(jnp.sum(state_f * target_f, axis=-1, keepdims=True))
    target_dot = lax.optimization_barrier(jnp.sum(target_f * target_f, axis=-1, keepdims=True))
    inv_state = lax.rsqrt(self_dot + EPS)
    inv_target = lax.rsqrt(target_dot + EPS)
    cosine = cross_dot * inv_state * inv_target
    return -LOSS_SCALE * (target_f * inv_state * inv_target - cosine * state_f * inv_state * inv_state)

def group_sum(left_groups, right_groups):

    def add_group(summed, operands):
        left_part, right_part = operands
        term = jnp.dot(left_part, right_part, preferred_element_type=jnp.float32).astype(jnp.bfloat16)
        term = lax.optimization_barrier(term)
        return (summed + term.astype(jnp.float32), None)
    init = jnp.zeros((left_groups.shape[0], right_groups.shape[2]), jnp.float32)
    summed, _ = lax.scan(add_group, init, (jnp.transpose(left_groups, (1, 0, 2)), right_groups))
    return summed

def reference(state_start, actions, targets, w_in, w_out, action_embed):
    hidden_cols = FF // N_COL
    w_in_groups = jnp.transpose(w_in.reshape(D, N_COL, hidden_cols), (1, 2, 0))
    w_out_groups = w_out.reshape(N_COL, hidden_cols, D)
    action_ids = jnp.arange(ACTIONS, dtype=jnp.int32)
    states = [state_start]
    pre_list = []
    hidden_list = []
    for unroll in range(UNROLL):
        current = states[-1]
        onehot = (actions[:, unroll][:, None] == action_ids[None, :]).astype(jnp.bfloat16)
        pre_act = jnp.dot(current, w_in, preferred_element_type=jnp.float32) + jnp.dot(onehot, action_embed, preferred_element_type=jnp.float32)
        hidden = jax.nn.silu(pre_act).astype(jnp.bfloat16)
        branch = group_sum(hidden.reshape(ROWS, N_COL, hidden_cols), w_out_groups)
        states.append((current.astype(jnp.float32) + branch).astype(jnp.bfloat16))
        pre_list.append(pre_act)
        hidden_list.append(hidden)
    state_grad = cosine_grad(states[UNROLL], targets[UNROLL - 1]).astype(jnp.bfloat16)
    grad_w_in = jnp.zeros((D, FF), jnp.float32)
    grad_w_out = jnp.zeros((FF, D), jnp.float32)
    for unroll in reversed(range(UNROLL)):
        back = jnp.dot(state_grad, w_out.T, preferred_element_type=jnp.float32)
        hid_grad = (back * silu_grad(pre_list[unroll])).astype(jnp.bfloat16)
        grad_w_out = grad_w_out + jnp.dot(hidden_list[unroll].T, state_grad, preferred_element_type=jnp.float32)
        grad_w_in = grad_w_in + jnp.dot(states[unroll].T, hid_grad, preferred_element_type=jnp.float32)
        if unroll > 0:
            input_part = group_sum(hid_grad.reshape(ROWS, N_COL, hidden_cols), w_in_groups)
            state_grad = (state_grad.astype(jnp.float32) + input_part + cosine_grad(states[unroll], targets[unroll - 1])).astype(jnp.bfloat16)
    return (grad_w_in, grad_w_out)
```

```python
import functools

import jax
import jax.numpy as jnp
from jax import lax
from jax.experimental import pallas as pl
from jax.experimental.pallas import tpu as pltpu
from jax.sharding import PartitionSpec as P

EPS = 1e-06
LOSS_SCALE = 128.0
MESH = pl.DeviceIdType.MESH
F32 = jnp.float32
BF16 = jnp.bfloat16


def silu_grad(pre_act):
    gate_val = jax.nn.sigmoid(pre_act)
    return gate_val * (1.0 + pre_act * (1.0 - gate_val))


def cosine_from(state_f, target_f, self_dot, cross_dot, target_dot):
    inv_state = lax.rsqrt(self_dot + EPS)
    inv_target = lax.rsqrt(target_dot + EPS)
    cosine = cross_dot * inv_state * inv_target
    return -LOSS_SCALE * (
        target_f * inv_state * inv_target - cosine * state_f * inv_state * inv_state
    )


def shared_cosine(state, target):
    state_f = state.astype(jnp.float32)
    target_f = target.astype(jnp.float32)
    self_dot, cross_dot, target_dot = lax.psum(
        (
            jnp.sum(state_f * state_f, axis=-1),
            jnp.sum(state_f * target_f, axis=-1),
            jnp.sum(target_f * target_f, axis=-1),
        ),
        "col",
    )
    return cosine_from(
        state_f, target_f, self_dot[:, None], cross_dot[:, None], target_dot[:, None]
    )


def gathered(state_start, actions, targets, w_in, w_out, action_embed):
    unroll_steps = targets.shape[0]
    col_width = state_start.shape[1]
    w_in_panel = lax.all_gather(w_in, "row", axis=0, tiled=True)
    w_out_panel = lax.all_gather(w_out, "row", axis=1, tiled=True)
    col_start = lax.axis_index("col") * col_width
    action_ids = jnp.arange(action_embed.shape[0], dtype=jnp.int32)
    contract_last = (((1,), (1,)), ((), ()))
    current = state_start
    full_states = []
    pre_list = []
    hidden_list = []
    cos_terms = []
    for unroll in range(unroll_steps):
        full_rows = lax.all_gather(current, "col", axis=1, tiled=True)
        onehot = (actions[:, unroll][:, None] == action_ids[None, :]).astype(jnp.bfloat16)
        pre_act = jnp.dot(full_rows, w_in_panel, preferred_element_type=jnp.float32) + jnp.dot(
            onehot, action_embed, preferred_element_type=jnp.float32
        )
        hidden = jax.nn.silu(pre_act).astype(jnp.bfloat16)
        partial_value = jnp.dot(hidden, w_out_panel, preferred_element_type=jnp.float32)
        target = targets[unroll]
        branch = lax.psum_scatter(
            partial_value.astype(jnp.bfloat16), "col", scatter_dimension=1, tiled=True
        ).astype(jnp.float32)
        current = (current.astype(jnp.float32) + branch).astype(jnp.bfloat16)
        target_slice = lax.dynamic_slice_in_dim(target, col_start, col_width, 1)
        cos_terms.append(shared_cosine(current, target_slice))
        full_states.append(full_rows)
        pre_list.append(pre_act)
        hidden_list.append(hidden)
    state_grad = cos_terms[unroll_steps - 1].astype(jnp.bfloat16)
    grad_list = [None] * unroll_steps
    hid_grads = [None] * unroll_steps
    for unroll in reversed(range(unroll_steps)):
        grad_rows = lax.all_gather(state_grad, "col", axis=1, tiled=True)
        back = lax.dot_general(
            grad_rows, w_out_panel, contract_last, preferred_element_type=jnp.float32
        )
        hid_grad = (back * silu_grad(pre_list[unroll])).astype(jnp.bfloat16)
        grad_list[unroll] = grad_rows
        hid_grads[unroll] = hid_grad
        if unroll > 0:
            input_part = lax.dot_general(
                hid_grad, w_in_panel, contract_last, preferred_element_type=jnp.float32
            )
            summed = lax.psum_scatter(
                input_part.astype(jnp.bfloat16), "col", scatter_dimension=1, tiled=True
            ).astype(jnp.float32)
            state_grad = (state_grad.astype(jnp.float32) + summed + cos_terms[unroll - 1]).astype(
                jnp.bfloat16
            )
    grad_stack = jnp.stack(grad_list)
    hidden_stack = jnp.stack(hidden_list)
    state_stack = jnp.stack(full_states)
    hid_stack = jnp.stack(hid_grads)
    grad_feature_blocks = lax.all_to_all(grad_stack, "row", split_axis=2, concat_axis=1, tiled=True)
    hidden_all = lax.all_gather(hidden_stack, "row", axis=1, tiled=True)
    grad_w_out = jnp.einsum(
        "kbf,kbd->fd", hidden_all, grad_feature_blocks, preferred_element_type=jnp.float32
    )
    state_feature_blocks = lax.all_to_all(
        state_stack, "row", split_axis=2, concat_axis=1, tiled=True
    )
    hid_all = lax.all_gather(hid_stack, "row", axis=1, tiled=True)
    grad_w_in = jnp.einsum(
        "kbd,kbf->df", state_feature_blocks, hid_all, preferred_element_type=jnp.float32
    )
    return (grad_w_in, grad_w_out)


CHUNKS = 4
STAGES = (
    ("into_hidden", 0, 0.0, 1.0),
    ("hidden", 0, 5.5, 2.4),
    ("other_terms", 0, 12.0, 1.0),
    ("next_state", 0, 16.0, 1.0),
    ("into_hidden", 1, 20.0, 1.0),
    ("hidden", 1, 25.5, 2.4),
    ("next_state", 1, 30.5, 2.4),
    ("last_grad", 1, 33.8, 2.4),
    ("into_back", 1, 38.0, 2.4),
    ("hidden_grad", 1, 43.5, 2.4),
    ("first_grad", 0, 48.0, 2.4),
    ("into_back", 0, 52.0, 2.4),
    ("hidden_grad", 0, 57.5, 2.4),
)


def stage_order():
    at = [
        (start + lag * k, i, k)
        for i, (_, _, start, lag) in enumerate(STAGES)
        for k in range(CHUNKS)
    ]
    return [(STAGES[i][0], STAGES[i][1], k) for _, i, k in sorted(at)]


def sem_plan(nc):
    at = {}
    total = 0
    for name, count in (
        [("wi", 1), ("wo", CHUNKS), ("s0x", 1), ("s0", nc), ("tg", 1)]
        + [(f"ag{i}", CHUNKS * nc) for i in range(3)]
        + [(f"z{i}", CHUNKS) for i in range(4)]
        + [(f"rs{i}", CHUNKS * nc) for i in range(3)]
        + [(f"dot{i}", CHUNKS * 4) for i in range(2)]
        + [(f"{n}b{u}", CHUNKS) for n in "hesg" for u in range(2)]
    ):
        at[name] = total
        total += count
    return at, total


def sends_in_all(nc):
    return 3 + CHUNKS + 2 * (nc - 1) + CHUNKS * (6 * (nc - 1) + 3 + 4 + 6 + 8)


def kernel(
    st, act, tg, wi, wo, emb, gwi, gwo,
    wix, wox, s0x, tgp, sf, gf, hf, ef, sb, gb, hb, eb, zs, zr, ys, cr, own, pre, ds, dz,
    send_sem, recv_sem,
):
    r, c = lax.axis_index("row"), lax.axis_index("col")
    nr, nc = 4, 8
    groups, piece, df = sf.shape[3], sf.shape[4], sf.shape[5]
    rows = groups * piece
    per = CHUNKS // 2
    sw = st.shape[3]
    a, b = lax.rem(r, 2), lax.div(r, 2)
    p, q = lax.div(c, 2), lax.rem(c, 2)
    near, far = r + 1 - 2 * a, lax.rem(r + 2, nr)
    twin = c + 1 - 2 * q
    at, _ = sem_plan(nc)
    started = []
    unused = iter(range(10000))

    def cpeer(o):
        return lax.rem(c + o, nc)

    def copy(src, dst, sem, slot, dev):
        return pltpu.make_async_remote_copy(
            src_ref=src, dst_ref=dst, send_sem=send_sem.at[sem], recv_sem=recv_sem.at[slot],
            device_id=dev, device_id_type=MESH,
        )

    def send(src, dst, slot, dev, when=None):
        sem = next(unused)
        started.append((src, dst, sem, slot, dev, when))
        if when is None:
            copy(src, dst, sem, slot, dev).start()
        else:
            pl.when(when)(lambda: copy(src, dst, sem, slot, dev).start())

    def arrived(dst, slot, when=None):
        if when is None:
            copy(dst, dst, 0, slot, (near, c)).wait_recv()
        else:
            pl.when(when)(lambda: copy(dst, dst, 0, slot, (near, c)).wait_recv())

    barrier = pltpu.get_barrier_semaphore()
    greeted = [(r, cpeer(o)) for o in range(1, nc)] + [
        (near, c), (far, c), (far, twin), (far, cpeer(nc // 2))
    ]
    for dev in greeted:
        pl.semaphore_signal(barrier, inc=1, device_id=dev, device_id_type=MESH)
    pl.semaphore_wait(barrier, len(greeted))

    home = lax.div(c, nc // 2) == b
    away = jnp.logical_not(home)
    send(st, s0x, at["s0x"], (far, cpeer(nc // 2)), away)
    send(wi, wix, at["wi"], (near, c))

    def place0(block, col):
        i = jnp.where(lax.div(col, nc // 2) == b, b, 1 - b)
        return sf.at[
            0, pl.ds(i * per, per), lax.rem(lax.div(col, 2), 2), :, :,
            pl.ds(pl.multiple_of(lax.rem(col, 2) * sw, sw), sw),
        ]

    for o in range(1, nc):
        send(st, place0(st, c), at["s0"] + c, (r, cpeer(o)), home)
    arrived(s0x, at["s0x"], away)
    for o in range(1, nc):
        send(s0x, place0(s0x, c), at["s0"] + c, (r, cpeer(o)), away)

    @pl.when(home)
    def _():
        place0(st, c)[...] = st[...]

    @pl.when(away)
    def _():
        place0(s0x, c)[...] = s0x[...]

    def send_wo(j):
        part = pl.ds(j * (wo.shape[0] // CHUNKS), wo.shape[0] // CHUNKS)
        send(wo.at[part], wox.at[part], at["wo"] + j, (near, c))

    send_wo(0)

    def mm(x, y, dims):
        return lax.dot_general(x, y, (dims, ((), ())), preferred_element_type=F32)

    def flat(x):
        return x.reshape(-1, x.shape[-1])

    ids = lax.broadcasted_iota(jnp.int32, (rows, emb.shape[0]), 1)
    plain, flipped, over_rows = ((1,), (0,)), ((1,), (1,)), ((0,), (0,))

    def spread(full, name, k):
        for o in range(1, nc):
            send(full.at[k, q, p], full.at[k, q, p], at[name] + k * nc + c, (r, cpeer(o)))

    def collect(full, name, k):
        for o in range(1, nc):
            j = cpeer(o)
            arrived(full.at[k, lax.rem(j, 2), lax.div(j, 2)], at[name] + k * nc + j)

    def exchange(phase, k, part):
        zs[phase, k] = part.astype(BF16)
        send(zs.at[phase, k], zr.at[phase, k], at[f"z{phase}"] + k, (far, c))

    def exchanged(phase, k):
        arrived(zr.at[phase, k], at[f"z{phase}"] + k)
        return zr[phase, k].astype(F32)

    def to_near(name, u, k, src, dst):
        send(src, dst.at[u, k], at[f"{name}b{u}"] + k, (near, c))

    def from_near(name, dst, u):
        for k in range(CHUNKS):
            arrived(dst.at[u, k], at[f"{name}b{u}"] + k)

    def terms(phase, k, left, weight, dims, which):
        ys[phase, k, which] = mm(left, weight[...], dims).astype(BF16).reshape(groups, piece, df)
        for o in range(groups - 1, -1, -1):
            g = lax.rem(p + o, groups)
            send(
                ys.at[phase, k, which, g], cr.at[phase, k, c], at[f"rs{phase}"] + k * nc + c,
                (r, 2 * g + which), which != q if o == 0 else None,
            )

    def total(phase, k):
        out = ys[phase, k, q, p].astype(F32)
        for o in range(1, nc):
            j = cpeer(o)
            arrived(cr.at[phase, k, j], at[f"rs{phase}"] + k * nc + j)
            out = out + cr[phase, k, j].astype(F32)
        return out

    lane = lax.broadcasted_iota(jnp.int32, (piece, 128), 1)

    def target(u, k):
        return tgp[k // per, u, k % per].astype(F32)

    def dots(u, k):
        s = own[u, k].astype(F32)
        t = target(u, k)
        ss = jnp.sum(s * s, axis=-1, keepdims=True)
        sc = jnp.sum(s * t, axis=-1, keepdims=True)
        tt = jnp.sum(t * t, axis=-1, keepdims=True)
        both = jnp.where(lane == 0, ss, jnp.where(lane == 1, sc, tt))
        me = 2 * b + q
        ds[u, k] = both
        dz[u, k, me] = both
        for dev in ((far, c), (far, twin), (r, twin)):
            send(ds.at[u, k], dz.at[u, k, me], at[f"dot{u}"] + k * 4 + me, dev)

    def dots_in(u, k):
        for o in range(1, 4):
            j = lax.rem(2 * b + q + o, 4)
            arrived(dz.at[u, k, j], at[f"dot{u}"] + k * 4 + j)

    def cosine(u, k):
        both = dz[u, k, 0]
        for j in range(1, 4):
            both = both + dz[u, k, j]
        return cosine_from(
            own[u, k].astype(F32), target(u, k), both[:, 0:1], both[:, 1:2], both[:, 2:3]
        )

    def into_hidden(u, k):
        if u > 0:
            collect(sf.at[u], "ag0", k)
        part = mm(flat(sf[u, k, a]), wi[...], plain)
        if u == 0 and k == 0:
            arrived(wix, at["wi"])
        part = part + mm(flat(sf[u, k, 1 - a]), wix[...], plain)
        act_k = act[rows * (k % per):rows * (k % per) + rows, u:u + 1]
        mine = jnp.where(k // per == b, 0, -emb.shape[0])
        onehot = (act_k + mine == ids).astype(F32).astype(BF16)
        part = part + mm(onehot, emb[...], plain)
        pre[u, k] = part
        exchange(u, k, part)
        if u == 0 and k < CHUNKS - 1:
            send_wo(k + 1)
        to_near("s", u, k, sf.at[u, k, 1 - a], sb)

    def hidden(u, k):
        v = pre[u, k] + exchanged(u, k)
        gate = jax.nn.sigmoid(v)
        hf[u, k] = (v * gate).astype(BF16)
        pre[u, k] = gate * (1.0 + v * (1.0 - gate))
        terms(u, k, hf[u, k], wo, plain, a)
        if u > 0:
            other_terms(u, k)

    def other_terms(u, k):
        if u == 0 and k == 0:
            for j in range(CHUNKS):
                part = pl.ds(j * (wo.shape[0] // CHUNKS), wo.shape[0] // CHUNKS)
                arrived(wox.at[part], at["wo"] + j)
        terms(u, k, hf[u, k], wox, plain, 1 - a)
        to_near("h", u, k, hf.at[u, k], hb)

    def next_state(u, k):
        new = (sf[u, k, q, p].astype(F32) + total(u, k)).astype(BF16)
        own[u, k] = new
        if u == 0:
            sf[1, k, q, p] = new
            spread(sf.at[1], "ag0", k)
        dots(u, k)

    def last_grad(u, k):
        dots_in(u, k)
        gf[1, k, q, p] = cosine(u, k).astype(BF16)
        spread(gf.at[1], "ag1", k)

    def into_back(u, k):
        collect(gf.at[u], f"ag{2 - u}", k)
        part = mm(flat(gf[u, k, a]), wo[...], flipped) + mm(
            flat(gf[u, k, 1 - a]), wox[...], flipped
        )
        back[k] = part
        exchange(3 - u, k, part)
        to_near("g", u, k, gf.at[u, k, 1 - a], gb)

    def hidden_grad(u, k):
        ef[u, k] = ((back[k] + exchanged(3 - u, k)) * pre[u, k]).astype(BF16)
        if u > 0:
            terms(2, k, ef[u, k], wi, flipped, a)
            terms(2, k, ef[u, k], wix, flipped, 1 - a)
        to_near("e", u, k, ef.at[u, k], eb)

    def first_grad(u, k):
        if k == 0:
            for j in range(CHUNKS):
                dots_in(0, j)
        summed = gf[1, k, q, p].astype(F32) + total(2, k) + cosine(0, k)
        gf[0, k, q, p] = summed.astype(BF16)
        spread(gf.at[0], "ag2", k)

    back = [None] * CHUNKS
    for o in range(1, nc):
        j = cpeer(o)
        arrived(place0(st, j), at["s0"] + j)

    def target_cols(plane_half):
        return pl.ds(pl.multiple_of((2 * plane_half + q) * df, df), df)

    send(
        tg.at[:, :, p, :, target_cols(1 - b)], tgp.at[b], at["tg"], (far, c)
    )
    tgp[b] = tg[:, :, p, :, target_cols(b)]
    run = dict(
        into_hidden=into_hidden, hidden=hidden, other_terms=other_terms, next_state=next_state,
        last_grad=last_grad, into_back=into_back, hidden_grad=hidden_grad, first_grad=first_grad,
    )
    for name, u, k in stage_order():
        if name == "next_state" and u == 0 and k == 0:
            arrived(tgp.at[1 - b], at["tg"])
        run[name](u, k)

    def out(acc, u, left, right, first):
        val = mm(left, right, over_rows)
        acc[...] = val if first else acc[...] + val

    def near_out(acc, u, left, right, first):
        out(acc, u, flat(left[u]), flat(right[u]), first)

    from_near("h", hb, 1)
    from_near("g", gb, 1)
    out(gwo, 1, flat(hf[1]), flat(gf[1, :, a]), True)
    near_out(gwo, 1, hb, gb, False)
    from_near("s", sb, 1)
    from_near("e", eb, 1)
    out(gwi, 1, flat(sf[1, :, a]), flat(ef[1]), True)
    near_out(gwi, 1, sb, eb, False)
    from_near("h", hb, 0)
    from_near("g", gb, 0)
    out(gwo, 0, flat(hf[0]), flat(gf[0, :, a]), False)
    near_out(gwo, 0, hb, gb, False)
    from_near("s", sb, 0)
    out(gwi, 0, flat(sf[0, :, a]), flat(ef[0]), False)
    from_near("e", eb, 0)
    near_out(gwi, 0, sb, eb, False)

    for src, dst, sem, slot, dev, when in started:
        if when is None:
            copy(src, dst, sem, slot, dev).wait_send()
        else:
            pl.when(when)(lambda: copy(src, dst, sem, slot, dev).wait_send())


def paired(nc, state_start, actions, targets, w_in, w_out, action_embed):
    rb, sw = state_start.shape
    df, fc = w_in.shape
    groups = nc // 2
    per = CHUNKS // 2
    piece = rb // (per * groups)
    rows = groups * piece
    vm = pl.BlockSpec(memory_space=pltpu.VMEM)
    _, receives = sem_plan(nc)
    state = pltpu.VMEM((2, CHUNKS, 2, groups, piece, df), BF16)
    hid = pltpu.VMEM((2, CHUNKS, rows, fc), BF16)
    feat = pltpu.VMEM((2, CHUNKS, rows, df), BF16)
    return pl.pallas_call(
        kernel,
        out_shape=(
            jax.ShapeDtypeStruct((df, fc), F32),
            jax.ShapeDtypeStruct((fc, df), F32),
        ),
        in_specs=[vm] * 6,
        out_specs=(vm, vm),
        scratch_shapes=[
            pltpu.VMEM((df, fc), BF16),
            pltpu.VMEM((fc, df), BF16),
            pltpu.VMEM((per, groups, piece, sw), BF16),
            pltpu.VMEM((2, 2, per, piece, df), BF16),
            state,
            state,
            hid,
            hid,
            pltpu.VMEM((2, CHUNKS, groups, piece, df), BF16),
            pltpu.VMEM((2, CHUNKS, groups, piece, df), BF16),
            hid,
            hid,
            pltpu.VMEM((4, CHUNKS, rows, fc), BF16),
            pltpu.VMEM((4, CHUNKS, rows, fc), BF16),
            pltpu.VMEM((3, CHUNKS, 2, groups, piece, df), BF16),
            pltpu.VMEM((3, CHUNKS, nc, piece, df), BF16),
            pltpu.VMEM((2, CHUNKS, piece, df), BF16),
            pltpu.VMEM((2, CHUNKS, rows, fc), F32),
            pltpu.VMEM((2, CHUNKS, piece, 128), F32),
            pltpu.VMEM((2, CHUNKS, 4, piece, 128), F32),
            pltpu.SemaphoreType.DMA((sends_in_all(nc),)),
            pltpu.SemaphoreType.DMA((receives,)),
        ],
        compiler_params=pltpu.CompilerParams(
            collective_id=0, has_side_effects=True, vmem_limit_bytes=56 * 1024 * 1024
        ),
    )(
        state_start.reshape(per, groups, piece, sw),
        actions,
        targets.reshape(targets.shape[0], per, groups, piece, targets.shape[2]),
        w_in,
        w_out,
        action_embed,
    )


def solution(mesh):
    nr, nc = mesh.shape["row"], mesh.shape["col"]

    def on_device(state_start, actions, targets, w_in, w_out, action_embed):
        rb, sw = state_start.shape
        fits = (
            targets.shape[0] == 2
            and nr == 4
            and nc == 8
            and rb % (16 * (CHUNKS // 2) * (nc // 2)) == 0
            and sw % 128 == 0
            and w_in.shape[0] == 2 * sw
            and w_in.shape[1] % (128 * CHUNKS) == 0
        )
        args = (state_start, actions, targets, w_in, w_out, action_embed)
        if fits:
            return paired(nc, *args)
        return gathered(*args)

    in_specs = (
        P("row", "col"),
        P("row", None),
        P(None, "row", None),
        P("row", "col"),
        P("col", "row"),
        P(None, "col"),
    )
    out_specs = (P("row", "col"), P("col", "row"))
    return jax.shard_map(
        on_device, mesh=mesh, in_specs=in_specs, out_specs=out_specs, check_vma=False
    )
```

```python
import functools

import jax
import jax.numpy as jnp
from jax import lax
from jax.experimental import pallas as pl
from jax.experimental.pallas import tpu as pltpu
from jax.sharding import PartitionSpec as P

EPS = 1e-06
LOSS_SCALE = 128.0
MESH = pl.DeviceIdType.MESH
F32 = jnp.float32
BF16 = jnp.bfloat16


def silu_grad(pre_act):
    gate_val = jax.nn.sigmoid(pre_act)
    return gate_val * (1.0 + pre_act * (1.0 - gate_val))


def cosine_from(state_f, target_f, self_dot, cross_dot, target_dot):
    inv_state = lax.rsqrt(self_dot + EPS)
    inv_target = lax.rsqrt(target_dot + EPS)
    cosine = cross_dot * inv_state * inv_target
    return -LOSS_SCALE * (
        target_f * inv_state * inv_target - cosine * state_f * inv_state * inv_state
    )


def shared_cosine(state, target):
    state_f = state.astype(jnp.float32)
    target_f = target.astype(jnp.float32)
    self_dot, cross_dot, target_dot = lax.psum(
        (
            jnp.sum(state_f * state_f, axis=-1),
            jnp.sum(state_f * target_f, axis=-1),
            jnp.sum(target_f * target_f, axis=-1),
        ),
        "col",
    )
    return cosine_from(
        state_f, target_f, self_dot[:, None], cross_dot[:, None], target_dot[:, None]
    )


def gathered(state_start, actions, targets, w_in, w_out, action_embed):
    unroll_steps = targets.shape[0]
    col_width = state_start.shape[1]
    w_in_panel = lax.all_gather(w_in, "row", axis=0, tiled=True)
    w_out_panel = lax.all_gather(w_out, "row", axis=1, tiled=True)
    col_start = lax.axis_index("col") * col_width
    action_ids = jnp.arange(action_embed.shape[0], dtype=jnp.int32)
    contract_last = (((1,), (1,)), ((), ()))
    current = state_start
    full_states = []
    pre_list = []
    hidden_list = []
    cos_terms = []
    for unroll in range(unroll_steps):
        full_rows = lax.all_gather(current, "col", axis=1, tiled=True)
        onehot = (actions[:, unroll][:, None] == action_ids[None, :]).astype(jnp.bfloat16)
        pre_act = jnp.dot(full_rows, w_in_panel, preferred_element_type=jnp.float32) + jnp.dot(
            onehot, action_embed, preferred_element_type=jnp.float32
        )
        hidden = jax.nn.silu(pre_act).astype(jnp.bfloat16)
        partial_value = jnp.dot(hidden, w_out_panel, preferred_element_type=jnp.float32)
        target = targets[unroll]
        branch = lax.psum_scatter(
            partial_value.astype(jnp.bfloat16), "col", scatter_dimension=1, tiled=True
        ).astype(jnp.float32)
        current = (current.astype(jnp.float32) + branch).astype(jnp.bfloat16)
        target_slice = lax.dynamic_slice_in_dim(target, col_start, col_width, 1)
        cos_terms.append(shared_cosine(current, target_slice))
        full_states.append(full_rows)
        pre_list.append(pre_act)
        hidden_list.append(hidden)
    state_grad = cos_terms[unroll_steps - 1].astype(jnp.bfloat16)
    grad_list = [None] * unroll_steps
    hid_grads = [None] * unroll_steps
    for unroll in reversed(range(unroll_steps)):
        grad_rows = lax.all_gather(state_grad, "col", axis=1, tiled=True)
        back = lax.dot_general(
            grad_rows, w_out_panel, contract_last, preferred_element_type=jnp.float32
        )
        hid_grad = (back * silu_grad(pre_list[unroll])).astype(jnp.bfloat16)
        grad_list[unroll] = grad_rows
        hid_grads[unroll] = hid_grad
        if unroll > 0:
            input_part = lax.dot_general(
                hid_grad, w_in_panel, contract_last, preferred_element_type=jnp.float32
            )
            summed = lax.psum_scatter(
                input_part.astype(jnp.bfloat16), "col", scatter_dimension=1, tiled=True
            ).astype(jnp.float32)
            state_grad = (state_grad.astype(jnp.float32) + summed + cos_terms[unroll - 1]).astype(
                jnp.bfloat16
            )
    grad_stack = jnp.stack(grad_list)
    hidden_stack = jnp.stack(hidden_list)
    state_stack = jnp.stack(full_states)
    hid_stack = jnp.stack(hid_grads)
    grad_feature_blocks = lax.all_to_all(grad_stack, "row", split_axis=2, concat_axis=1, tiled=True)
    hidden_all = lax.all_gather(hidden_stack, "row", axis=1, tiled=True)
    grad_w_out = jnp.einsum(
        "kbf,kbd->fd", hidden_all, grad_feature_blocks, preferred_element_type=jnp.float32
    )
    state_feature_blocks = lax.all_to_all(
        state_stack, "row", split_axis=2, concat_axis=1, tiled=True
    )
    hid_all = lax.all_gather(hid_stack, "row", axis=1, tiled=True)
    grad_w_in = jnp.einsum(
        "kbd,kbf->df", state_feature_blocks, hid_all, preferred_element_type=jnp.float32
    )
    return (grad_w_in, grad_w_out)


CHUNKS = 4
STAGES = (
    ("into_hidden", 0, 0.0, 1.0),
    ("hidden", 0, 5.5, 2.4),
    ("other_terms", 0, 12.0, 1.0),
    ("next_state", 0, 16.0, 1.0),
    ("into_hidden", 1, 20.0, 1.0),
    ("hidden", 1, 25.5, 2.4),
    ("next_state", 1, 30.5, 2.4),
    ("last_grad", 1, 33.8, 2.4),
    ("into_back", 1, 38.0, 2.4),
    ("hidden_grad", 1, 43.5, 2.4),
    ("first_grad", 0, 48.0, 2.4),
    ("into_back", 0, 52.0, 2.4),
    ("hidden_grad", 0, 57.5, 2.4),
)


def stage_order():
    at = [
        (start + lag * k, i, k)
        for i, (_, _, start, lag) in enumerate(STAGES)
        for k in range(CHUNKS)
    ]
    return [(STAGES[i][0], STAGES[i][1], k) for _, i, k in sorted(at)]


def sem_plan(nc):
    at = {}
    total = 0
    for name, count in (
        [("wi", 1), ("wo", CHUNKS), ("s0x", 1), ("s0", nc), ("tg", 1)]
        + [(f"{n}t{u}", CHUNKS) for n in "sg" for u in range(2)]
        + [(f"ag{i}", CHUNKS * nc) for i in range(3)]
        + [(f"z{i}", CHUNKS) for i in range(4)]
        + [(f"rs{i}", CHUNKS * nc) for i in range(3)]
        + [(f"dot{i}", CHUNKS * 4) for i in range(2)]
        + [(f"{n}b{u}", CHUNKS) for n in "hesg" for u in range(2)]
    ):
        at[name] = total
        total += count
    return at, total


def sends_in_all(nc):
    return 3 + CHUNKS + 2 * nc + CHUNKS * (6 * (nc - 1) + 3 + 4 + 6 + 8 + 4)


def kernel(
    st, act_in, tg, wi_in, wo_in, emb_in, gwi_out, gwo_out,
    wi, wo, act, emb, gwi, gwo, wix, wox, s0x, tgp, sf, gf, hf, ef, sb, gb, hb, eb, zs, zr, ys, cr, own, pre, ds, dz,
    send_sem, recv_sem, load_sem,
):
    r, c = lax.axis_index("row"), lax.axis_index("col")
    nr, nc = 4, 8
    groups, piece, df = sf.shape[3], sf.shape[4], sf.shape[5]
    rows = groups * piece
    per = CHUNKS // 2
    sw = st.shape[3]
    a, b = lax.rem(r, 2), lax.div(r, 2)
    p, q = lax.div(c, 2), lax.rem(c, 2)
    near, far = r + 1 - 2 * a, lax.rem(r + 2, nr)
    twin = c + 1 - 2 * q
    at, _ = sem_plan(nc)
    started = []
    unused = iter(range(10000))

    def cpeer(o):
        return lax.rem(c + o, nc)

    def copy(src, dst, sem, slot, dev):
        return pltpu.make_async_remote_copy(
            src_ref=src, dst_ref=dst, send_sem=send_sem.at[sem], recv_sem=recv_sem.at[slot],
            device_id=dev, device_id_type=MESH,
        )

    def send(src, dst, slot, dev, when=None):
        sem = next(unused)
        started.append((src, dst, sem, slot, dev, when))
        if when is None:
            copy(src, dst, sem, slot, dev).start()
        else:
            pl.when(when)(lambda: copy(src, dst, sem, slot, dev).start())

    def arrived(dst, slot, when=None):
        if when is None:
            copy(dst, dst, 0, slot, (near, c)).wait_recv()
        else:
            pl.when(when)(lambda: copy(dst, dst, 0, slot, (near, c)).wait_recv())

    home = lax.div(c, nc // 2) == b
    away = jnp.logical_not(home)

    def place0(col):
        i = jnp.where(lax.div(col, nc // 2) == b, b, 1 - b)
        return sf.at[
            0, pl.ds(i * per, per), lax.rem(lax.div(col, 2), 2), :, :,
            pl.ds(pl.multiple_of(lax.rem(col, 2) * sw, sw), sw),
        ]

    def target_cols(plane_half):
        return pl.ds(pl.multiple_of((2 * plane_half + q) * df, df), df)

    loads = [
        pltpu.make_async_copy(src, dst, load_sem.at[i])
        for i, (src, dst) in enumerate((
            (wi_in, wi), (act_in, act), (emb_in, emb), (wo_in, wo),
            (tg.at[:, :, p, :, target_cols(b)], tgp.at[b]),
        ))
    ]
    keep = pltpu.make_async_copy(st, place0(c), load_sem.at[5])
    for load in loads:
        load.start()
    pl.when(home)(lambda: keep.start())
    gwo_store = pltpu.make_async_copy(gwo, gwo_out, load_sem.at[6])
    gwi_store = pltpu.make_async_copy(gwi, gwi_out, load_sem.at[7])

    barrier = pltpu.get_barrier_semaphore()
    greeted = [(r, cpeer(o)) for o in range(1, nc)] + [
        (near, c), (far, c), (far, twin), (far, cpeer(nc // 2))
    ]
    for dev in greeted:
        pl.semaphore_signal(barrier, inc=1, device_id=dev, device_id_type=MESH)
    pl.semaphore_wait(barrier, len(greeted))

    send(st, s0x, at["s0x"], (far, cpeer(nc // 2)), away)
    for o in (nc // 2, 2, nc - 2):
        send(st, place0(c), at["s0"] + c, (r, cpeer(o)), home)
    send(st, place0(c), at["s0"] + c, (r, twin), home)
    send(wi_in, wix, at["wi"], (near, c))

    def send_wo(j):
        part = pl.ds(j * (wo.shape[0] // CHUNKS), wo.shape[0] // CHUNKS)
        send(wo_in.at[part], wox.at[part], at["wo"] + j, (near, c))

    send_wo(0)
    arrived(s0x, at["s0x"], away)
    for o in (nc // 2, 2, nc - 2):
        send(s0x, place0(c), at["s0"] + c, (r, cpeer(o)), away)
    send(s0x, place0(c), at["s0"] + c, (r, twin), away)

    @pl.when(away)
    def _():
        place0(c)[...] = s0x[...]

    for o in (nc // 2, 2, nc - 2):
        j = cpeer(o)
        arrived(place0(j), at["s0"] + j)
        send(place0(j), place0(j), at["s0"] + j, (r, twin))
    pl.when(home)(lambda: keep.wait())

    def mm(x, y, dims):
        return lax.dot_general(x, y, (dims, ((), ())), preferred_element_type=F32)

    def flat(x):
        return x.reshape(-1, x.shape[-1])

    ids = lax.broadcasted_iota(jnp.int32, (emb.shape[0], per * rows), 0)
    plain, flipped, over_rows = ((1,), (0,)), ((1,), (1,)), ((0,), (0,))

    def spread(full, name, k):
        for o in range(1, nc):
            send(full.at[k, q, p], full.at[k, q, p], at[name] + k * nc + c, (r, cpeer(o)))

    def collect(full, name, k):
        for o in range(1, nc):
            j = cpeer(o)
            arrived(full.at[k, lax.rem(j, 2), lax.div(j, 2)], at[name] + k * nc + j)

    def exchange(phase, k, part):
        zs[phase, k] = part.astype(BF16)
        send(zs.at[phase, k], zr.at[phase, k], at[f"z{phase}"] + k, (far, c))

    def exchanged(phase, k):
        arrived(zr.at[phase, k], at[f"z{phase}"] + k)
        return zr[phase, k].astype(F32)

    def to_near(name, u, k, src, dst):
        send(src, dst.at[u, k], at[f"{name}b{u}"] + k, (near, c))

    mine = pl.ds(q * (groups // 2), groups // 2)
    others = pl.ds((1 - q) * (groups // 2), groups // 2)

    def half_to_near(name, u, k, src, dst):
        send(src.at[u, k, 1 - a, mine], dst.at[u, k, mine], at[f"{name}b{u}"] + k, (near, c))

    def half_to_twin(name, u, k, dst):
        arrived(dst.at[u, k, mine], at[f"{name}b{u}"] + k)
        send(dst.at[u, k, mine], dst.at[u, k, mine], at[f"{name}t{u}"] + k, (r, twin))

    def from_twin(name, dst, u):
        for k in range(CHUNKS):
            arrived(dst.at[u, k, others], at[f"{name}t{u}"] + k)

    def from_near(name, dst, u):
        for k in range(CHUNKS):
            arrived(dst.at[u, k], at[f"{name}b{u}"] + k)

    def terms(phase, k, left, weight, dims, which):
        ys[phase, k, which] = mm(left, weight[...], dims).astype(BF16).reshape(groups, piece, df)
        for o in range(groups - 1, -1, -1):
            g = lax.rem(p + o, groups)
            send(
                ys.at[phase, k, which, g], cr.at[phase, k, c], at[f"rs{phase}"] + k * nc + c,
                (r, 2 * g + which), which != q if o == 0 else None,
            )

    def total(phase, k):
        out = ys[phase, k, q, p].astype(F32)
        for o in range(1, nc):
            j = cpeer(o)
            arrived(cr.at[phase, k, j], at[f"rs{phase}"] + k * nc + j)
            out = out + cr[phase, k, j].astype(F32)
        return out

    lane = lax.broadcasted_iota(jnp.int32, (piece, 128), 1)

    def target(u, k):
        return tgp[k // per, u, k % per].astype(F32)

    def dots(u, k):
        s = own[u, k].astype(F32)
        t = target(u, k)
        ss = jnp.sum(s * s, axis=-1, keepdims=True)
        sc = jnp.sum(s * t, axis=-1, keepdims=True)
        tt = jnp.sum(t * t, axis=-1, keepdims=True)
        both = jnp.where(lane == 0, ss, jnp.where(lane == 1, sc, tt))
        me = 2 * b + q
        ds[u, k] = both
        dz[u, k, me] = both
        for dev in ((far, c), (far, twin), (r, twin)):
            send(ds.at[u, k], dz.at[u, k, me], at[f"dot{u}"] + k * 4 + me, dev)

    def dots_in(u, k):
        for o in range(1, 4):
            j = lax.rem(2 * b + q + o, 4)
            arrived(dz.at[u, k, j], at[f"dot{u}"] + k * 4 + j)

    def cosine(u, k):
        both = dz[u, k, 0]
        for j in range(1, 4):
            both = both + dz[u, k, j]
        return cosine_from(
            own[u, k].astype(F32), target(u, k), both[:, 0:1], both[:, 1:2], both[:, 2:3]
        )

    def into_hidden(u, k):
        if u > 0:
            collect(sf.at[u], "ag0", k)
        part = mm(flat(sf[u, k, a]), wi[...], plain)
        if u == 0 and k == 0:
            arrived(wix, at["wi"])
        part = part + mm(flat(sf[u, k, 1 - a]), wix[...], plain)
        part = part + acts[u][rows * (k % per):rows * (k % per) + rows] * jnp.where(k // per == b, 1.0, 0.0)
        pre[u, k] = part
        exchange(u, k, part)
        if u == 0 and k < CHUNKS - 1:
            send_wo(k + 1)
        if u == 0 and k == CHUNKS - 1:
            send(
                tg.at[:, :, p, :, target_cols(1 - b)], tgp.at[b], at["tg"], (far, c)
            )
        if u == 1:
            to_near("h", 0, k, hf.at[0, k], hb)

    def hidden(u, k):
        v = pre[u, k] + exchanged(u, k)
        gate = jax.nn.sigmoid(v)
        hf[u, k] = (v * gate).astype(BF16)
        pre[u, k] = gate * (1.0 + v * (1.0 - gate))
        terms(u, k, hf[u, k], wo, plain, a)
        if u > 0:
            other_terms(u, k)

    def other_terms(u, k):
        if u == 0 and k == 0:
            for j in range(CHUNKS):
                part = pl.ds(j * (wo.shape[0] // CHUNKS), wo.shape[0] // CHUNKS)
                arrived(wox.at[part], at["wo"] + j)
        terms(u, k, hf[u, k], wox, plain, 1 - a)
        if u == 1:
            to_near("h", 1, k, hf.at[1, k], hb)

    def next_state(u, k):
        new = (sf[u, k, q, p].astype(F32) + total(u, k)).astype(BF16)
        own[u, k] = new
        if u == 0:
            sf[1, k, q, p] = new
            spread(sf.at[1], "ag0", k)
        dots(u, k)

    def last_grad(u, k):
        dots_in(u, k)
        gf[1, k, q, p] = cosine(u, k).astype(BF16)
        spread(gf.at[1], "ag1", k)

    def into_back(u, k):
        collect(gf.at[u], f"ag{2 - u}", k)
        part = mm(flat(gf[u, k, a]), wo[...], flipped) + mm(
            flat(gf[u, k, 1 - a]), wox[...], flipped
        )
        back[k] = part
        exchange(3 - u, k, part)
        for v in range(2):
            if u == 1:
                half_to_near("s", v, k, sf, sb)
            else:
                half_to_near("g", v, k, gf, gb)

    def hidden_grad(u, k):
        ef[u, k] = ((back[k] + exchanged(3 - u, k)) * pre[u, k]).astype(BF16)
        if u > 0:
            terms(2, k, ef[u, k], wi, flipped, a)
            terms(2, k, ef[u, k], wix, flipped, 1 - a)
        to_near("e", u, k, ef.at[u, k], eb)

    def first_grad(u, k):
        for v in range(2):
            half_to_twin("s", v, k, sb)
        if k == 0:
            for j in range(CHUNKS):
                dots_in(0, j)
        summed = gf[1, k, q, p].astype(F32) + total(2, k) + cosine(0, k)
        gf[0, k, q, p] = summed.astype(BF16)
        spread(gf.at[0], "ag2", k)

    back = [None] * CHUNKS
    for o in (nc // 2, 2, nc - 2):
        j = cpeer(o)
        j = j + 1 - 2 * q
        arrived(place0(j), at["s0"] + j)
    arrived(place0(twin), at["s0"] + twin)
    for load in loads[:3]:
        load.wait()
    acts = [
        mm((act[u:u + 1] == ids).astype(F32).astype(BF16), emb[...], over_rows) for u in range(2)
    ]
    run = dict(
        into_hidden=into_hidden, hidden=hidden, other_terms=other_terms, next_state=next_state,
        last_grad=last_grad, into_back=into_back, hidden_grad=hidden_grad, first_grad=first_grad,
    )
    for name, u, k in stage_order():
        if name == "next_state" and u == 0 and k == 0:
            arrived(tgp.at[1 - b], at["tg"])
            loads[4].wait()
        if name == "hidden" and u == 0 and k == 0:
            loads[3].wait()
        run[name](u, k)

    def out(acc, u, left, right, first):
        val = mm(left, right, over_rows)
        acc[...] = val if first else acc[...] + val

    def near_out(acc, u, left, right, first):
        out(acc, u, flat(left[u]), flat(right[u]), first)

    for u in range(2):
        for k in range(CHUNKS):
            half_to_twin("g", u, k, gb)
    from_near("h", hb, 1)
    from_near("h", hb, 0)
    out(gwo, 1, flat(hf[1]), flat(gf[1, :, a]), True)
    out(gwo, 0, flat(hf[0]), flat(gf[0, :, a]), False)
    from_twin("g", gb, 1)
    from_twin("g", gb, 0)
    near_out(gwo, 1, hb, gb, False)
    near_out(gwo, 0, hb, gb, False)
    gwo_store.start()
    from_twin("s", sb, 1)
    from_twin("s", sb, 0)
    from_near("e", eb, 1)
    out(gwi, 1, flat(sf[1, :, a]), flat(ef[1]), True)
    out(gwi, 0, flat(sf[0, :, a]), flat(ef[0]), False)
    near_out(gwi, 1, sb, eb, False)

    for src, dst, sem, slot, dev, when in started:
        if when is None:
            copy(src, dst, sem, slot, dev).wait_send()
        else:
            pl.when(when)(lambda: copy(src, dst, sem, slot, dev).wait_send())
    from_near("e", eb, 0)
    near_out(gwi, 0, sb, eb, False)
    gwi_store.start()
    gwo_store.wait()
    gwi_store.wait()


def paired(nc, state_start, actions, targets, w_in, w_out, action_embed):
    rb, sw = state_start.shape
    df, fc = w_in.shape
    groups = nc // 2
    per = CHUNKS // 2
    piece = rb // (per * groups)
    rows = groups * piece
    hbm = pl.BlockSpec(memory_space=pltpu.HBM)
    _, receives = sem_plan(nc)
    state = pltpu.VMEM((2, CHUNKS, 2, groups, piece, df), BF16)
    hid = pltpu.VMEM((2, CHUNKS, rows, fc), BF16)
    feat = pltpu.VMEM((2, CHUNKS, rows, df), BF16)
    return pl.pallas_call(
        kernel,
        out_shape=(
            jax.ShapeDtypeStruct((df, fc), F32),
            jax.ShapeDtypeStruct((fc, df), F32),
        ),
        in_specs=[hbm] * 6,
        out_specs=(hbm, hbm),
        scratch_shapes=[
            pltpu.VMEM((df, fc), BF16),
            pltpu.VMEM((fc, df), BF16),
            pltpu.VMEM((2, rb), jnp.int32),
            pltpu.VMEM(action_embed.shape, BF16),
            pltpu.VMEM((df, fc), F32),
            pltpu.VMEM((fc, df), F32),
            pltpu.VMEM((df, fc), BF16),
            pltpu.VMEM((fc, df), BF16),
            pltpu.VMEM((per, groups, piece, sw), BF16),
            pltpu.VMEM((2, 2, per, piece, df), BF16),
            state,
            state,
            hid,
            hid,
            pltpu.VMEM((2, CHUNKS, groups, piece, df), BF16),
            pltpu.VMEM((2, CHUNKS, groups, piece, df), BF16),
            hid,
            hid,
            pltpu.VMEM((4, CHUNKS, rows, fc), BF16),
            pltpu.VMEM((4, CHUNKS, rows, fc), BF16),
            pltpu.VMEM((3, CHUNKS, 2, groups, piece, df), BF16),
            pltpu.VMEM((3, CHUNKS, nc, piece, df), BF16),
            pltpu.VMEM((2, CHUNKS, piece, df), BF16),
            pltpu.VMEM((2, CHUNKS, rows, fc), F32),
            pltpu.VMEM((2, CHUNKS, piece, 128), F32),
            pltpu.VMEM((2, CHUNKS, 4, piece, 128), F32),
            pltpu.SemaphoreType.DMA((sends_in_all(nc),)),
            pltpu.SemaphoreType.DMA((receives,)),
            pltpu.SemaphoreType.DMA((8,)),
        ],
        compiler_params=pltpu.CompilerParams(
            collective_id=0, has_side_effects=True, vmem_limit_bytes=56 * 1024 * 1024
        ),
    )(
        state_start.reshape(per, groups, piece, sw),
        actions.T,
        targets.reshape(targets.shape[0], per, groups, piece, targets.shape[2]),
        w_in,
        w_out,
        action_embed,
    )


def solution(mesh):
    nr, nc = mesh.shape["row"], mesh.shape["col"]

    def on_device(state_start, actions, targets, w_in, w_out, action_embed):
        rb, sw = state_start.shape
        fits = (
            targets.shape[0] == 2
            and nr == 4
            and nc == 8
            and rb % (16 * (CHUNKS // 2) * (nc // 2)) == 0
            and sw % 128 == 0
            and w_in.shape[0] == 2 * sw
            and w_in.shape[1] % (128 * CHUNKS) == 0
        )
        args = (state_start, actions, targets, w_in, w_out, action_embed)
        if fits:
            return paired(nc, *args)
        return gathered(*args)

    in_specs = (
        P("row", "col"),
        P("row", None),
        P(None, "row", None),
        P("row", "col"),
        P("col", "row"),
        P(None, "col"),
    )
    out_specs = (P("row", "col"), P("col", "row"))
    return jax.shard_map(
        on_device, mesh=mesh, in_specs=in_specs, out_specs=out_specs, check_vma=False
    )
```

```python
import functools

import jax
import jax.numpy as jnp
from jax import lax
from jax.experimental import pallas as pl
from jax.experimental.pallas import tpu as pltpu
from jax.sharding import PartitionSpec as P

EPS = 1e-06
LOSS_SCALE = 128.0
MESH = pl.DeviceIdType.MESH
F32 = jnp.float32
BF16 = jnp.bfloat16


def silu_grad(pre_act):
    gate_val = jax.nn.sigmoid(pre_act)
    return gate_val * (1.0 + pre_act * (1.0 - gate_val))


def cosine_from(state_f, target_f, self_dot, cross_dot, target_dot):
    inv_state = lax.rsqrt(self_dot + EPS)
    inv_target = lax.rsqrt(target_dot + EPS)
    cosine = cross_dot * inv_state * inv_target
    return -LOSS_SCALE * (
        target_f * inv_state * inv_target - cosine * state_f * inv_state * inv_state
    )


def shared_cosine(state, target):
    state_f = state.astype(jnp.float32)
    target_f = target.astype(jnp.float32)
    self_dot, cross_dot, target_dot = lax.psum(
        (
            jnp.sum(state_f * state_f, axis=-1),
            jnp.sum(state_f * target_f, axis=-1),
            jnp.sum(target_f * target_f, axis=-1),
        ),
        "col",
    )
    return cosine_from(
        state_f, target_f, self_dot[:, None], cross_dot[:, None], target_dot[:, None]
    )


def gathered(state_start, actions, targets, w_in, w_out, action_embed):
    unroll_steps = targets.shape[0]
    col_width = state_start.shape[1]
    w_in_panel = lax.all_gather(w_in, "row", axis=0, tiled=True)
    w_out_panel = lax.all_gather(w_out, "row", axis=1, tiled=True)
    col_start = lax.axis_index("col") * col_width
    action_ids = jnp.arange(action_embed.shape[0], dtype=jnp.int32)
    contract_last = (((1,), (1,)), ((), ()))
    current = state_start
    full_states = []
    pre_list = []
    hidden_list = []
    cos_terms = []
    for unroll in range(unroll_steps):
        full_rows = lax.all_gather(current, "col", axis=1, tiled=True)
        onehot = (actions[:, unroll][:, None] == action_ids[None, :]).astype(jnp.bfloat16)
        pre_act = jnp.dot(full_rows, w_in_panel, preferred_element_type=jnp.float32) + jnp.dot(
            onehot, action_embed, preferred_element_type=jnp.float32
        )
        hidden = jax.nn.silu(pre_act).astype(jnp.bfloat16)
        partial_value = jnp.dot(hidden, w_out_panel, preferred_element_type=jnp.float32)
        target = targets[unroll]
        branch = lax.psum_scatter(
            partial_value.astype(jnp.bfloat16), "col", scatter_dimension=1, tiled=True
        ).astype(jnp.float32)
        current = (current.astype(jnp.float32) + branch).astype(jnp.bfloat16)
        target_slice = lax.dynamic_slice_in_dim(target, col_start, col_width, 1)
        cos_terms.append(shared_cosine(current, target_slice))
        full_states.append(full_rows)
        pre_list.append(pre_act)
        hidden_list.append(hidden)
    state_grad = cos_terms[unroll_steps - 1].astype(jnp.bfloat16)
    grad_list = [None] * unroll_steps
    hid_grads = [None] * unroll_steps
    for unroll in reversed(range(unroll_steps)):
        grad_rows = lax.all_gather(state_grad, "col", axis=1, tiled=True)
        back = lax.dot_general(
            grad_rows, w_out_panel, contract_last, preferred_element_type=jnp.float32
        )
        hid_grad = (back * silu_grad(pre_list[unroll])).astype(jnp.bfloat16)
        grad_list[unroll] = grad_rows
        hid_grads[unroll] = hid_grad
        if unroll > 0:
            input_part = lax.dot_general(
                hid_grad, w_in_panel, contract_last, preferred_element_type=jnp.float32
            )
            summed = lax.psum_scatter(
                input_part.astype(jnp.bfloat16), "col", scatter_dimension=1, tiled=True
            ).astype(jnp.float32)
            state_grad = (state_grad.astype(jnp.float32) + summed + cos_terms[unroll - 1]).astype(
                jnp.bfloat16
            )
    grad_stack = jnp.stack(grad_list)
    hidden_stack = jnp.stack(hidden_list)
    state_stack = jnp.stack(full_states)
    hid_stack = jnp.stack(hid_grads)
    grad_feature_blocks = lax.all_to_all(grad_stack, "row", split_axis=2, concat_axis=1, tiled=True)
    hidden_all = lax.all_gather(hidden_stack, "row", axis=1, tiled=True)
    grad_w_out = jnp.einsum(
        "kbf,kbd->fd", hidden_all, grad_feature_blocks, preferred_element_type=jnp.float32
    )
    state_feature_blocks = lax.all_to_all(
        state_stack, "row", split_axis=2, concat_axis=1, tiled=True
    )
    hid_all = lax.all_gather(hid_stack, "row", axis=1, tiled=True)
    grad_w_in = jnp.einsum(
        "kbd,kbf->df", state_feature_blocks, hid_all, preferred_element_type=jnp.float32
    )
    return (grad_w_in, grad_w_out)


CHUNKS = 4
STAGES = (
    ("into_hidden", 0, 0.0, 1.0),
    ("hidden", 0, 5.5, 2.4),
    ("other_terms", 0, 12.0, 1.0),
    ("next_state", 0, 16.0, 1.0),
    ("into_hidden", 1, 20.0, 1.0),
    ("hidden", 1, 25.5, 2.4),
    ("next_state", 1, 30.5, 2.4),
    ("last_grad", 1, 33.8, 2.4),
    ("into_back", 1, 38.0, 2.4),
    ("hidden_grad", 1, 43.5, 2.4),
    ("first_grad", 0, 48.0, 2.4),
    ("into_back", 0, 52.0, 2.4),
    ("hidden_grad", 0, 57.5, 2.4),
)


def stage_order():
    at = [
        (start + lag * k, i, k)
        for i, (_, _, start, lag) in enumerate(STAGES)
        for k in range(CHUNKS)
    ]
    return [(STAGES[i][0], STAGES[i][1], k) for _, i, k in sorted(at)]


def sem_plan(nc):
    at = {}
    total = 0
    for name, count in (
        [("wi", 1), ("wo", CHUNKS), ("s0x", 1), ("s0", nc), ("tg", 1)]
        + [(f"{n}t{u}", CHUNKS) for n in "sg" for u in range(2)]
        + [(f"{n}p{u}", 4) for n in "sg" for u in range(2)]
        + [(f"ag{i}", CHUNKS * nc) for i in range(3)]
        + [(f"z{i}", CHUNKS) for i in range(4)]
        + [(f"rs{i}", CHUNKS * nc) for i in range(3)]
        + [(f"dot{i}", CHUNKS * 4) for i in range(2)]
        + [(f"{n}b{u}", CHUNKS) for n in "hesg" for u in range(2)]
    ):
        at[name] = total
        total += count
    return at, total


def sends_in_all(nc):
    return 3 + CHUNKS + 2 * nc + CHUNKS * (6 * (nc - 1) + 3 + 4 + 6 + 8 + 4) + 12


def kernel(
    st, act_in, tg, wi_in, wo_in, emb_in, gwi_out, gwo_out,
    wi, wo, act, emb, gwi, gwo, wix, wox, s0x, tgp, sf, gf, hf, ef, sb, gb, hb, eb, zs, zr, ys, cr, own, pre, ds, dz,
    send_sem, recv_sem, load_sem,
):
    r, c = lax.axis_index("row"), lax.axis_index("col")
    nr, nc = 4, 8
    groups, piece, df = sf.shape[3], sf.shape[4], sf.shape[5]
    rows = groups * piece
    per = CHUNKS // 2
    sw = st.shape[3]
    a, b = lax.rem(r, 2), lax.div(r, 2)
    p, q = lax.div(c, 2), lax.rem(c, 2)
    near, far = r + 1 - 2 * a, lax.rem(r + 2, nr)
    twin = c + 1 - 2 * q
    at, _ = sem_plan(nc)
    started = []
    unused = iter(range(10000))

    def toggled(v, bits):
        for bit in (1, 2, 4):
            if bits & bit:
                v = v + bit - 2 * bit * lax.rem(lax.div(v, bit), 2)
        return v

    def cpeer(o):
        return toggled(c, (6, 7, 4, 5, 2, 3, 1)[o - 1])

    def copy(src, dst, sem, slot, dev):
        return pltpu.make_async_remote_copy(
            src_ref=src, dst_ref=dst, send_sem=send_sem.at[sem], recv_sem=recv_sem.at[slot],
            device_id=dev, device_id_type=MESH,
        )

    def send(src, dst, slot, dev, when=None):
        sem = next(unused)
        started.append((src, dst, sem, slot, dev, when))
        if when is None:
            copy(src, dst, sem, slot, dev).start()
        else:
            pl.when(when)(lambda: copy(src, dst, sem, slot, dev).start())

    def arrived(dst, slot, when=None):
        if when is None:
            copy(dst, dst, 0, slot, (near, c)).wait_recv()
        else:
            pl.when(when)(lambda: copy(dst, dst, 0, slot, (near, c)).wait_recv())

    home = lax.div(c, nc // 2) == b
    away = jnp.logical_not(home)

    def place0(col):
        i = jnp.where(lax.div(col, nc // 2) == b, b, 1 - b)
        return sf.at[
            0, pl.ds(i * per, per), lax.rem(lax.div(col, 2), 2), :, :,
            pl.ds(pl.multiple_of(lax.rem(col, 2) * sw, sw), sw),
        ]

    def target_cols(plane_half):
        return pl.ds(pl.multiple_of((2 * plane_half + q) * df, df), df)

    loads = [
        pltpu.make_async_copy(src, dst, load_sem.at[i])
        for i, (src, dst) in enumerate((
            (wi_in, wi), (act_in, act), (emb_in, emb), (wo_in, wo),
            (tg.at[:, :, p, :, target_cols(b)], tgp.at[b]),
        ))
    ]
    keep = pltpu.make_async_copy(st, place0(c), load_sem.at[5])
    for load in loads:
        load.start()
    pl.when(home)(lambda: keep.start())
    gwo_store = pltpu.make_async_copy(gwo, gwo_out, load_sem.at[6])
    gwi_store = pltpu.make_async_copy(gwi, gwi_out, load_sem.at[7])

    barrier = pltpu.get_barrier_semaphore()
    greeted = [(r, cpeer(o)) for o in range(1, nc)] + [
        (near, c), (far, c), (far, twin), (far, toggled(c, 4))
    ]
    for dev in greeted:
        pl.semaphore_signal(barrier, inc=1, device_id=dev, device_id_type=MESH)
    pl.semaphore_wait(barrier, len(greeted))

    send(st, s0x, at["s0x"], (far, toggled(c, 4)), away)
    for o in (6, 4, 2):
        send(st, place0(c), at["s0"] + c, (r, toggled(c, o)), home)
    send(st, place0(c), at["s0"] + c, (r, twin), home)
    send(wi_in, wix, at["wi"], (near, c))

    def send_wo(j):
        part = pl.ds(j * (wo.shape[0] // CHUNKS), wo.shape[0] // CHUNKS)
        send(wo_in.at[part], wox.at[part], at["wo"] + j, (near, c))

    send_wo(0)
    arrived(s0x, at["s0x"], away)
    for o in (6, 4, 2):
        send(s0x, place0(c), at["s0"] + c, (r, toggled(c, o)), away)
    send(s0x, place0(c), at["s0"] + c, (r, twin), away)

    @pl.when(away)
    def _():
        place0(c)[...] = s0x[...]

    for o in (4, 2, 6):
        j = toggled(c, o)
        arrived(place0(j), at["s0"] + j)
        send(place0(j), place0(j), at["s0"] + j, (r, twin))
    pl.when(home)(lambda: keep.wait())

    def mm(x, y, dims):
        return lax.dot_general(x, y, (dims, ((), ())), preferred_element_type=F32)

    def flat(x):
        return x.reshape(-1, x.shape[-1])

    ids = lax.broadcasted_iota(jnp.int32, (emb.shape[0], per * rows), 0)
    plain, flipped, over_rows = ((1,), (0,)), ((1,), (1,)), ((0,), (0,))

    def spread(full, name, k):
        for o in range(1, nc):
            send(full.at[k, q, p], full.at[k, q, p], at[name] + k * nc + c, (r, cpeer(o)))

    def collect(full, name, k):
        for o in range(1, nc):
            j = cpeer(o)
            arrived(full.at[k, lax.rem(j, 2), lax.div(j, 2)], at[name] + k * nc + j)

    def exchange(phase, k, part):
        zs[phase, k] = part.astype(BF16)
        send(zs.at[phase, k], zr.at[phase, k], at[f"z{phase}"] + k, (far, c))

    def exchanged(phase, k):
        arrived(zr.at[phase, k], at[f"z{phase}"] + k)
        return zr[phase, k].astype(F32)

    def to_near(name, u, k, src, dst):
        send(src, dst.at[u, k], at[f"{name}b{u}"] + k, (near, c))

    mine = pl.ds(q * (groups // 2), groups // 2)
    others = pl.ds((1 - q) * (groups // 2), groups // 2)

    def half_to_near(name, u, k, src, dst):
        send(src.at[u, k, 1 - a, mine], dst.at[u, k, mine], at[f"{name}b{u}"] + k, (near, c))

    def half_to_twin(name, u, k, dst):
        arrived(dst.at[u, k, mine], at[f"{name}b{u}"] + k)
        send(dst.at[u, k, mine], dst.at[u, k, mine], at[f"{name}t{u}"] + k, (r, twin))

    def piece_to_near(name, u, k, src, dst):
        send(src.at[k, q, p], dst.at[u, k, p], at[f"{name}b{u}"] + k, (near, c), q != a)

    def share(name, u, dst):
        for k in range(CHUNKS):
            arrived(dst.at[u, k, p], at[f"{name}b{u}"] + k, q == a)
        for o in (6, 4, 2):
            send(dst.at[u, :, p], dst.at[u, :, p], at[f"{name}p{u}"] + p, (r, toggled(c, o)), q == a)

    def complete(name, u, dst):
        for o in (1, 2, 3):
            g = toggled(p, o)
            arrived(dst.at[u, :, g], at[f"{name}p{u}"] + g, q == a)
        send(dst.at[u], dst.at[u], at[f"{name}t{u}"], (r, twin), q == a)

    def completed(name, u, dst):
        arrived(dst.at[u], at[f"{name}t{u}"], q != a)

    def from_twin(name, dst, u):
        for k in range(CHUNKS):
            arrived(dst.at[u, k, others], at[f"{name}t{u}"] + k)

    def from_near(name, dst, u):
        for k in range(CHUNKS):
            arrived(dst.at[u, k], at[f"{name}b{u}"] + k)

    def terms(phase, k, left, weight, dims, which):
        ys[phase, k, which] = mm(left, weight[...], dims).astype(BF16).reshape(groups, piece, df)
        for o in range(groups - 1, -1, -1):
            g = toggled(p, o)
            send(
                ys.at[phase, k, which, g], cr.at[phase, k, c], at[f"rs{phase}"] + k * nc + c,
                (r, 2 * g + which), which != q if o == 0 else None,
            )

    def total(phase, k):
        out = ys[phase, k, q, p].astype(F32)
        for o in range(1, nc):
            j = cpeer(o)
            arrived(cr.at[phase, k, j], at[f"rs{phase}"] + k * nc + j)
            out = out + cr[phase, k, j].astype(F32)
        return out

    lane = lax.broadcasted_iota(jnp.int32, (piece, 128), 1)

    def target(u, k):
        return tgp[k // per, u, k % per].astype(F32)

    def dots(u, k):
        s = own[u, k].astype(F32)
        t = target(u, k)
        ss = jnp.sum(s * s, axis=-1, keepdims=True)
        sc = jnp.sum(s * t, axis=-1, keepdims=True)
        tt = jnp.sum(t * t, axis=-1, keepdims=True)
        both = jnp.where(lane == 0, ss, jnp.where(lane == 1, sc, tt))
        me = 2 * b + q
        ds[u, k] = both
        dz[u, k, me] = both
        for dev in ((far, c), (far, twin), (r, twin)):
            send(ds.at[u, k], dz.at[u, k, me], at[f"dot{u}"] + k * 4 + me, dev)

    def dots_in(u, k):
        for o in range(1, 4):
            j = lax.rem(2 * b + q + o, 4)
            arrived(dz.at[u, k, j], at[f"dot{u}"] + k * 4 + j)

    def cosine(u, k):
        both = dz[u, k, 0]
        for j in range(1, 4):
            both = both + dz[u, k, j]
        return cosine_from(
            own[u, k].astype(F32), target(u, k), both[:, 0:1], both[:, 1:2], both[:, 2:3]
        )

    def into_hidden(u, k):
        if u > 0:
            collect(sf.at[u], "ag0", k)
        part = mm(flat(sf[u, k, a]), wi[...], plain)
        if u == 0 and k == 0:
            arrived(wix, at["wi"])
        part = part + mm(flat(sf[u, k, 1 - a]), wix[...], plain)
        part = part + acts[u][rows * (k % per):rows * (k % per) + rows] * jnp.where(k // per == b, 1.0, 0.0)
        pre[u, k] = part
        exchange(u, k, part)
        if u == 0 and k < CHUNKS - 1:
            send_wo(k + 1)
        if u == 0 and k == CHUNKS - 1:
            send(
                tg.at[:, :, p, :, target_cols(1 - b)], tgp.at[b], at["tg"], (far, c)
            )
        if u == 1:
            to_near("h", 0, k, hf.at[0, k], hb)

    def hidden(u, k):
        v = pre[u, k] + exchanged(u, k)
        gate = jax.nn.sigmoid(v)
        hf[u, k] = (v * gate).astype(BF16)
        pre[u, k] = gate * (1.0 + v * (1.0 - gate))
        terms(u, k, hf[u, k], wo, plain, a)
        if u > 0:
            other_terms(u, k)

    def other_terms(u, k):
        if u == 0 and k == 0:
            for j in range(CHUNKS):
                part = pl.ds(j * (wo.shape[0] // CHUNKS), wo.shape[0] // CHUNKS)
                arrived(wox.at[part], at["wo"] + j)
        terms(u, k, hf[u, k], wox, plain, 1 - a)
        if u == 1:
            to_near("h", 1, k, hf.at[1, k], hb)

    def next_state(u, k):
        new = (sf[u, k, q, p].astype(F32) + total(u, k)).astype(BF16)
        own[u, k] = new
        if u == 0:
            sf[1, k, q, p] = new
            spread(sf.at[1], "ag0", k)
            piece_to_near("s", 1, k, sf.at[1], sb)
        dots(u, k)

    def last_grad(u, k):
        dots_in(u, k)
        gf[1, k, q, p] = cosine(u, k).astype(BF16)
        spread(gf.at[1], "ag1", k)
        piece_to_near("g", 1, k, gf.at[1], gb)

    def into_back(u, k):
        collect(gf.at[u], f"ag{2 - u}", k)
        part = mm(flat(gf[u, k, a]), wo[...], flipped) + mm(
            flat(gf[u, k, 1 - a]), wox[...], flipped
        )
        back[k] = part
        exchange(3 - u, k, part)
        if u == 1:
            half_to_near("s", 0, k, sf, sb)

    def hidden_grad(u, k):
        ef[u, k] = ((back[k] + exchanged(3 - u, k)) * pre[u, k]).astype(BF16)
        if u > 0:
            terms(2, k, ef[u, k], wi, flipped, a)
            terms(2, k, ef[u, k], wix, flipped, 1 - a)
        to_near("e", u, k, ef.at[u, k], eb)

    def first_grad(u, k):
        half_to_twin("s", 0, k, sb)
        if k == 0:
            for j in range(CHUNKS):
                dots_in(0, j)
        summed = gf[1, k, q, p].astype(F32) + total(2, k) + cosine(0, k)
        gf[0, k, q, p] = summed.astype(BF16)
        spread(gf.at[0], "ag2", k)
        piece_to_near("g", 0, k, gf.at[0], gb)

    back = [None] * CHUNKS
    for o in (4, 2, 6):
        j = toggled(c, o)
        j = j + 1 - 2 * q
        arrived(place0(j), at["s0"] + j)
    arrived(place0(twin), at["s0"] + twin)
    for load in loads[:3]:
        load.wait()
    acts = [
        mm((act[u:u + 1] == ids).astype(F32).astype(BF16), emb[...], over_rows) for u in range(2)
    ]
    run = dict(
        into_hidden=into_hidden, hidden=hidden, other_terms=other_terms, next_state=next_state,
        last_grad=last_grad, into_back=into_back, hidden_grad=hidden_grad, first_grad=first_grad,
    )
    for name, u, k in stage_order():
        if name == "next_state" and u == 0 and k == 0:
            arrived(tgp.at[1 - b], at["tg"])
            loads[4].wait()
        if name == "hidden" and u == 0 and k == 0:
            loads[3].wait()
        run[name](u, k)
        if k == CHUNKS - 1:
            if name == "into_hidden" and u == 1:
                share("s", 1, sb)
            elif name == "into_back" and u == 1:
                complete("s", 1, sb)
                share("g", 1, gb)
            elif name == "into_back" and u == 0:
                complete("g", 1, gb)
                share("g", 0, gb)

    def out(acc, u, left, right, first):
        val = mm(left, right, over_rows)
        acc[...] = val if first else acc[...] + val

    def near_out(acc, u, left, right, first):
        out(acc, u, flat(left[u]), flat(right[u]), first)

    complete("g", 0, gb)
    from_near("h", hb, 1)
    from_near("h", hb, 0)
    out(gwo, 1, flat(hf[1]), flat(gf[1, :, a]), True)
    out(gwo, 0, flat(hf[0]), flat(gf[0, :, a]), False)
    completed("g", 1, gb)
    completed("g", 0, gb)
    near_out(gwo, 1, hb, gb, False)
    near_out(gwo, 0, hb, gb, False)
    gwo_store.start()
    completed("s", 1, sb)
    from_twin("s", sb, 0)
    from_near("e", eb, 1)
    out(gwi, 1, flat(sf[1, :, a]), flat(ef[1]), True)
    out(gwi, 0, flat(sf[0, :, a]), flat(ef[0]), False)
    near_out(gwi, 1, sb, eb, False)

    for src, dst, sem, slot, dev, when in started:
        if when is None:
            copy(src, dst, sem, slot, dev).wait_send()
        else:
            pl.when(when)(lambda: copy(src, dst, sem, slot, dev).wait_send())
    from_near("e", eb, 0)
    near_out(gwi, 0, sb, eb, False)
    gwi_store.start()
    gwo_store.wait()
    gwi_store.wait()


def paired(nc, state_start, actions, targets, w_in, w_out, action_embed):
    rb, sw = state_start.shape
    df, fc = w_in.shape
    groups = nc // 2
    per = CHUNKS // 2
    piece = rb // (per * groups)
    rows = groups * piece
    hbm = pl.BlockSpec(memory_space=pltpu.HBM)
    _, receives = sem_plan(nc)
    state = pltpu.VMEM((2, CHUNKS, 2, groups, piece, df), BF16)
    hid = pltpu.VMEM((2, CHUNKS, rows, fc), BF16)
    feat = pltpu.VMEM((2, CHUNKS, rows, df), BF16)
    return pl.pallas_call(
        kernel,
        out_shape=(
            jax.ShapeDtypeStruct((df, fc), F32),
            jax.ShapeDtypeStruct((fc, df), F32),
        ),
        in_specs=[hbm] * 6,
        out_specs=(hbm, hbm),
        scratch_shapes=[
            pltpu.VMEM((df, fc), BF16),
            pltpu.VMEM((fc, df), BF16),
            pltpu.VMEM((2, rb), jnp.int32),
            pltpu.VMEM(action_embed.shape, BF16),
            pltpu.VMEM((df, fc), F32),
            pltpu.VMEM((fc, df), F32),
            pltpu.VMEM((df, fc), BF16),
            pltpu.VMEM((fc, df), BF16),
            pltpu.VMEM((per, groups, piece, sw), BF16),
            pltpu.VMEM((2, 2, per, piece, df), BF16),
            state,
            state,
            hid,
            hid,
            pltpu.VMEM((2, CHUNKS, groups, piece, df), BF16),
            pltpu.VMEM((2, CHUNKS, groups, piece, df), BF16),
            hid,
            hid,
            pltpu.VMEM((4, CHUNKS, rows, fc), BF16),
            pltpu.VMEM((4, CHUNKS, rows, fc), BF16),
            pltpu.VMEM((3, CHUNKS, 2, groups, piece, df), BF16),
            pltpu.VMEM((3, CHUNKS, nc, piece, df), BF16),
            pltpu.VMEM((2, CHUNKS, piece, df), BF16),
            pltpu.VMEM((2, CHUNKS, rows, fc), F32),
            pltpu.VMEM((2, CHUNKS, piece, 128), F32),
            pltpu.VMEM((2, CHUNKS, 4, piece, 128), F32),
            pltpu.SemaphoreType.DMA((sends_in_all(nc),)),
            pltpu.SemaphoreType.DMA((receives,)),
            pltpu.SemaphoreType.DMA((8,)),
        ],
        compiler_params=pltpu.CompilerParams(
            collective_id=0, has_side_effects=True, vmem_limit_bytes=56 * 1024 * 1024
        ),
    )(
        state_start.reshape(per, groups, piece, sw),
        actions.T,
        targets.reshape(targets.shape[0], per, groups, piece, targets.shape[2]),
        w_in,
        w_out,
        action_embed,
    )


def solution(mesh):
    nr, nc = mesh.shape["row"], mesh.shape["col"]

    def on_device(state_start, actions, targets, w_in, w_out, action_embed):
        rb, sw = state_start.shape
        fits = (
            targets.shape[0] == 2
            and nr == 4
            and nc == 8
            and rb % (16 * (CHUNKS // 2) * (nc // 2)) == 0
            and sw % 128 == 0
            and w_in.shape[0] == 2 * sw
            and w_in.shape[1] % (128 * CHUNKS) == 0
        )
        args = (state_start, actions, targets, w_in, w_out, action_embed)
        if fits:
            return paired(nc, *args)
        return gathered(*args)

    in_specs = (
        P("row", "col"),
        P("row", None),
        P(None, "row", None),
        P("row", "col"),
        P("col", "row"),
        P(None, "col"),
    )
    out_specs = (P("row", "col"), P("col", "row"))
    return jax.shard_map(
        on_device, mesh=mesh, in_specs=in_specs, out_specs=out_specs, check_vma=False
    )
```

```python
import functools

import jax
import jax.numpy as jnp
from jax import lax
from jax.experimental import pallas as pl
from jax.experimental.pallas import tpu as pltpu
from jax.sharding import PartitionSpec as P

EPS = 1e-06
LOSS_SCALE = 128.0
MESH = pl.DeviceIdType.MESH
F32 = jnp.float32
BF16 = jnp.bfloat16


def silu_grad(pre_act):
    gate_val = jax.nn.sigmoid(pre_act)
    return gate_val * (1.0 + pre_act * (1.0 - gate_val))


def cosine_from(state_f, target_f, self_dot, cross_dot, target_dot):
    inv_state = lax.rsqrt(self_dot + EPS)
    inv_target = lax.rsqrt(target_dot + EPS)
    cosine = cross_dot * inv_state * inv_target
    return -LOSS_SCALE * (
        target_f * inv_state * inv_target - cosine * state_f * inv_state * inv_state
    )


def shared_cosine(state, target):
    state_f = state.astype(jnp.float32)
    target_f = target.astype(jnp.float32)
    self_dot, cross_dot, target_dot = lax.psum(
        (
            jnp.sum(state_f * state_f, axis=-1),
            jnp.sum(state_f * target_f, axis=-1),
            jnp.sum(target_f * target_f, axis=-1),
        ),
        "col",
    )
    return cosine_from(
        state_f, target_f, self_dot[:, None], cross_dot[:, None], target_dot[:, None]
    )


def gathered(state_start, actions, targets, w_in, w_out, action_embed):
    unroll_steps = targets.shape[0]
    col_width = state_start.shape[1]
    w_in_panel = lax.all_gather(w_in, "row", axis=0, tiled=True)
    w_out_panel = lax.all_gather(w_out, "row", axis=1, tiled=True)
    col_start = lax.axis_index("col") * col_width
    action_ids = jnp.arange(action_embed.shape[0], dtype=jnp.int32)
    contract_last = (((1,), (1,)), ((), ()))
    current = state_start
    full_states = []
    pre_list = []
    hidden_list = []
    cos_terms = []
    for unroll in range(unroll_steps):
        full_rows = lax.all_gather(current, "col", axis=1, tiled=True)
        onehot = (actions[:, unroll][:, None] == action_ids[None, :]).astype(jnp.bfloat16)
        pre_act = jnp.dot(full_rows, w_in_panel, preferred_element_type=jnp.float32) + jnp.dot(
            onehot, action_embed, preferred_element_type=jnp.float32
        )
        hidden = jax.nn.silu(pre_act).astype(jnp.bfloat16)
        partial_value = jnp.dot(hidden, w_out_panel, preferred_element_type=jnp.float32)
        target = targets[unroll]
        branch = lax.psum_scatter(
            partial_value.astype(jnp.bfloat16), "col", scatter_dimension=1, tiled=True
        ).astype(jnp.float32)
        current = (current.astype(jnp.float32) + branch).astype(jnp.bfloat16)
        target_slice = lax.dynamic_slice_in_dim(target, col_start, col_width, 1)
        cos_terms.append(shared_cosine(current, target_slice))
        full_states.append(full_rows)
        pre_list.append(pre_act)
        hidden_list.append(hidden)
    state_grad = cos_terms[unroll_steps - 1].astype(jnp.bfloat16)
    grad_list = [None] * unroll_steps
    hid_grads = [None] * unroll_steps
    for unroll in reversed(range(unroll_steps)):
        grad_rows = lax.all_gather(state_grad, "col", axis=1, tiled=True)
        back = lax.dot_general(
            grad_rows, w_out_panel, contract_last, preferred_element_type=jnp.float32
        )
        hid_grad = (back * silu_grad(pre_list[unroll])).astype(jnp.bfloat16)
        grad_list[unroll] = grad_rows
        hid_grads[unroll] = hid_grad
        if unroll > 0:
            input_part = lax.dot_general(
                hid_grad, w_in_panel, contract_last, preferred_element_type=jnp.float32
            )
            summed = lax.psum_scatter(
                input_part.astype(jnp.bfloat16), "col", scatter_dimension=1, tiled=True
            ).astype(jnp.float32)
            state_grad = (state_grad.astype(jnp.float32) + summed + cos_terms[unroll - 1]).astype(
                jnp.bfloat16
            )
    grad_stack = jnp.stack(grad_list)
    hidden_stack = jnp.stack(hidden_list)
    state_stack = jnp.stack(full_states)
    hid_stack = jnp.stack(hid_grads)
    grad_feature_blocks = lax.all_to_all(grad_stack, "row", split_axis=2, concat_axis=1, tiled=True)
    hidden_all = lax.all_gather(hidden_stack, "row", axis=1, tiled=True)
    grad_w_out = jnp.einsum(
        "kbf,kbd->fd", hidden_all, grad_feature_blocks, preferred_element_type=jnp.float32
    )
    state_feature_blocks = lax.all_to_all(
        state_stack, "row", split_axis=2, concat_axis=1, tiled=True
    )
    hid_all = lax.all_gather(hid_stack, "row", axis=1, tiled=True)
    grad_w_in = jnp.einsum(
        "kbd,kbf->df", state_feature_blocks, hid_all, preferred_element_type=jnp.float32
    )
    return (grad_w_in, grad_w_out)


CHUNKS = 4
STAGES = (
    ("into_hidden", 0, 0.0, 1.0),
    ("hidden", 0, 5.5, 2.4),
    ("other_terms", 0, 12.0, 1.0),
    ("next_state", 0, 16.0, 1.0),
    ("into_hidden", 1, 20.0, 1.0),
    ("hidden", 1, 25.5, 2.4),
    ("next_state", 1, 30.5, 2.4),
    ("last_grad", 1, 33.8, 2.4),
    ("into_back", 1, 38.0, 2.4),
    ("hidden_grad", 1, 43.5, 2.4),
    ("first_grad", 0, 48.0, 2.4),
    ("into_back", 0, 52.0, 2.4),
    ("hidden_grad", 0, 57.5, 2.4),
)


def stage_order():
    at = [
        (start + lag * k, i, k)
        for i, (_, _, start, lag) in enumerate(STAGES)
        for k in range(CHUNKS)
    ]
    return [(STAGES[i][0], STAGES[i][1], k) for _, i, k in sorted(at)]


def sem_plan(nc):
    at = {}
    total = 0
    for name, count in (
        [("wi", 1), ("wo", CHUNKS), ("s0x", 1), ("s0", nc), ("tg", 1)]
        + [(f"{n}t{u}", CHUNKS) for n in "sg" for u in range(2)]
        + [(f"{n}p{u}", 4) for n in "sg" for u in range(2)]
        + [(f"ag{i}", CHUNKS * nc) for i in range(3)]
        + [(f"z{i}", CHUNKS) for i in range(4)]
        + [(f"rs{i}", CHUNKS * nc) for i in range(3)]
        + [(f"dot{i}", CHUNKS * 4) for i in range(2)]
        + [(f"{n}b{u}", CHUNKS) for n in "hesg" for u in range(2)]
    ):
        at[name] = total
        total += count
    return at, total


def sends_in_all(nc):
    return 3 + CHUNKS + 2 * nc + CHUNKS * (6 * (nc - 1) + 3 + 4 + 6 + 8 + 4) + 12


def kernel(
    st, act_in, tg, wi_in, wo_in, emb_in, gwi_out, gwo_out,
    wi, wo, act, emb, gwi, gwo, wix, wox, s0x, tgp, sf, gf, hf, ef, sb, gb, hb, eb, zs, zr, ys, cr, own, pre, ds, dz,
    send_sem, recv_sem, load_sem,
):
    r, c = lax.axis_index("row"), lax.axis_index("col")
    nr, nc = 4, 8
    groups, piece, df = sf.shape[3], sf.shape[4], sf.shape[5]
    rows = groups * piece
    per = CHUNKS // 2
    sw = st.shape[3]
    a, b = lax.rem(r, 2), lax.div(r, 2)
    p, q = lax.div(c, 2), lax.rem(c, 2)
    near, far = r + 1 - 2 * a, lax.rem(r + 2, nr)
    twin = c + 1 - 2 * q
    at, _ = sem_plan(nc)
    started = []
    unused = iter(range(10000))

    def toggled(v, bits):
        for bit in (1, 2, 4):
            if bits & bit:
                v = v + bit - 2 * bit * lax.rem(lax.div(v, bit), 2)
        return v

    def cpeer(o):
        return toggled(c, (6, 7, 4, 5, 2, 3, 1)[o - 1])

    def copy(src, dst, sem, slot, dev):
        return pltpu.make_async_remote_copy(
            src_ref=src, dst_ref=dst, send_sem=send_sem.at[sem], recv_sem=recv_sem.at[slot],
            device_id=dev, device_id_type=MESH,
        )

    def send(src, dst, slot, dev, when=None):
        sem = next(unused)
        started.append((src, dst, sem, slot, dev, when))
        if when is None:
            copy(src, dst, sem, slot, dev).start()
        else:
            pl.when(when)(lambda: copy(src, dst, sem, slot, dev).start())

    def arrived(dst, slot, when=None):
        if when is None:
            copy(dst, dst, 0, slot, (near, c)).wait_recv()
        else:
            pl.when(when)(lambda: copy(dst, dst, 0, slot, (near, c)).wait_recv())

    home = lax.div(c, nc // 2) == b
    away = jnp.logical_not(home)

    def place0(col):
        i = jnp.where(lax.div(col, nc // 2) == b, b, 1 - b)
        return sf.at[
            0, pl.ds(i * per, per), lax.rem(lax.div(col, 2), 2), :, :,
            pl.ds(pl.multiple_of(lax.rem(col, 2) * sw, sw), sw),
        ]

    def target_cols(plane_half):
        return pl.ds(pl.multiple_of((2 * plane_half + q) * df, df), df)

    loads = [
        pltpu.make_async_copy(src, dst, load_sem.at[i])
        for i, (src, dst) in enumerate((
            (wi_in, wi), (act_in, act), (emb_in, emb), (wo_in, wo),
            (tg.at[:, :, p, :, target_cols(b)], tgp.at[b]),
        ))
    ]
    keep = pltpu.make_async_copy(st, place0(c), load_sem.at[5])
    for load in loads:
        load.start()
    pl.when(home)(lambda: keep.start())
    gwo_store = pltpu.make_async_copy(gwo, gwo_out, load_sem.at[6])
    gwi_store = pltpu.make_async_copy(gwi, gwi_out, load_sem.at[7])

    barrier = pltpu.get_barrier_semaphore()
    greeted = [(r, cpeer(o)) for o in range(1, nc)] + [
        (near, c), (far, c), (far, twin), (far, toggled(c, 4))
    ]
    for dev in greeted:
        pl.semaphore_signal(barrier, inc=1, device_id=dev, device_id_type=MESH)
    pl.semaphore_wait(barrier, len(greeted))

    send(st, s0x, at["s0x"], (far, toggled(c, 4)), away)
    for o in (6, 4, 2):
        send(st, place0(c), at["s0"] + c, (r, toggled(c, o)), home)
    send(st, place0(c), at["s0"] + c, (r, twin), home)
    send(wi_in, wix, at["wi"], (near, c))

    def send_wo(j):
        part = pl.ds(j * (wo.shape[0] // CHUNKS), wo.shape[0] // CHUNKS)
        send(wo_in.at[part], wox.at[part], at["wo"] + j, (near, c))

    send_wo(0)
    arrived(s0x, at["s0x"], away)
    for o in (6, 4, 2):
        send(s0x, place0(c), at["s0"] + c, (r, toggled(c, o)), away)
    send(s0x, place0(c), at["s0"] + c, (r, twin), away)

    @pl.when(away)
    def _():
        place0(c)[...] = s0x[...]

    for o in (4, 2, 6):
        j = toggled(c, o)
        arrived(place0(j), at["s0"] + j)
        send(place0(j), place0(j), at["s0"] + j, (r, twin))
    pl.when(home)(lambda: keep.wait())

    def mm(x, y, dims):
        return lax.dot_general(x, y, (dims, ((), ())), preferred_element_type=F32)

    def flat(x):
        return x.reshape(-1, x.shape[-1])

    ids = lax.broadcasted_iota(jnp.int32, (emb.shape[0], per * rows), 0)
    plain, flipped, over_rows = ((1,), (0,)), ((1,), (1,)), ((0,), (0,))

    def spread(full, name, k):
        for o in range(1, nc):
            send(full.at[k, q, p], full.at[k, q, p], at[name] + k * nc + c, (r, cpeer(o)))

    def collect(full, name, k):
        for o in range(1, nc):
            j = cpeer(o)
            arrived(full.at[k, lax.rem(j, 2), lax.div(j, 2)], at[name] + k * nc + j)

    def exchange(phase, k, part):
        zs[phase, k] = part.astype(BF16)
        send(zs.at[phase, k], zr.at[phase, k], at[f"z{phase}"] + k, (far, c))

    def exchanged(phase, k):
        arrived(zr.at[phase, k], at[f"z{phase}"] + k)
        return zr[phase, k].astype(F32)

    def to_near(name, u, k, src, dst):
        send(src, dst.at[u, k], at[f"{name}b{u}"] + k, (near, c))

    mine = pl.ds(q * (groups // 2), groups // 2)
    others = pl.ds((1 - q) * (groups // 2), groups // 2)

    def half_to_near(name, u, k, src, dst):
        send(src.at[u, k, 1 - a, mine], dst.at[u, k, mine], at[f"{name}b{u}"] + k, (near, c))

    def half_to_twin(name, u, k, dst):
        arrived(dst.at[u, k, mine], at[f"{name}b{u}"] + k)
        send(dst.at[u, k, mine], dst.at[u, k, mine], at[f"{name}t{u}"] + k, (r, twin))

    def piece_to_near(name, u, k, src, dst):
        send(src.at[k, q, p], dst.at[u, k, p], at[f"{name}b{u}"] + k, (near, c), q != a)

    def share(name, u, dst):
        for k in range(CHUNKS):
            arrived(dst.at[u, k, p], at[f"{name}b{u}"] + k, q == a)
        for o in (6, 4, 2):
            send(dst.at[u, :, p], dst.at[u, :, p], at[f"{name}p{u}"] + p, (r, toggled(c, o)), q == a)

    def complete(name, u, dst):
        for o in (1, 2, 3):
            g = toggled(p, o)
            arrived(dst.at[u, :, g], at[f"{name}p{u}"] + g, q == a)
        send(dst.at[u], dst.at[u], at[f"{name}t{u}"], (r, twin), q == a)

    def completed(name, u, dst):
        arrived(dst.at[u], at[f"{name}t{u}"], q != a)

    def from_twin(name, dst, u):
        for k in range(CHUNKS):
            arrived(dst.at[u, k, others], at[f"{name}t{u}"] + k)

    def from_near(name, dst, u):
        for k in range(CHUNKS):
            arrived(dst.at[u, k], at[f"{name}b{u}"] + k)

    def terms(phase, k, left, weight, dims, which):
        ys[phase, k, which] = mm(left, weight[...], dims).astype(BF16).reshape(groups, piece, df)
        for o in range(groups - 1, -1, -1):
            g = toggled(p, o)
            send(
                ys.at[phase, k, which, g], cr.at[phase, k, c], at[f"rs{phase}"] + k * nc + c,
                (r, 2 * g + which), which != q if o == 0 else None,
            )

    def total(phase, k):
        out = ys[phase, k, q, p].astype(F32)
        for o in range(1, nc):
            j = cpeer(o)
            arrived(cr.at[phase, k, j], at[f"rs{phase}"] + k * nc + j)
            out = out + cr[phase, k, j].astype(F32)
        return out

    lane = lax.broadcasted_iota(jnp.int32, (piece, 128), 1)

    def target(u, k):
        return tgp[k // per, u, k % per].astype(F32)

    def dots(u, k):
        s = own[u, k].astype(F32)
        t = target(u, k)
        ss = jnp.sum(s * s, axis=-1, keepdims=True)
        sc = jnp.sum(s * t, axis=-1, keepdims=True)
        tt = jnp.sum(t * t, axis=-1, keepdims=True)
        both = jnp.where(lane == 0, ss, jnp.where(lane == 1, sc, tt))
        me = 2 * b + q
        ds[u, k] = both
        dz[u, k, me] = both
        for dev in ((far, c), (far, twin), (r, twin)):
            send(ds.at[u, k], dz.at[u, k, me], at[f"dot{u}"] + k * 4 + me, dev)

    def dots_in(u, k):
        for o in range(1, 4):
            j = lax.rem(2 * b + q + o, 4)
            arrived(dz.at[u, k, j], at[f"dot{u}"] + k * 4 + j)

    def cosine(u, k):
        both = dz[u, k, 0]
        for j in range(1, 4):
            both = both + dz[u, k, j]
        return cosine_from(
            own[u, k].astype(F32), target(u, k), both[:, 0:1], both[:, 1:2], both[:, 2:3]
        )

    def into_hidden(u, k):
        if u > 0:
            collect(sf.at[u], "ag0", k)
        part = mm(flat(sf[u, k, a]), wi[...], plain)
        if u == 0 and k == 0:
            arrived(wix, at["wi"])
        part = part + mm(flat(sf[u, k, 1 - a]), wix[...], plain)
        part = part + acts[u][rows * (k % per):rows * (k % per) + rows] * jnp.where(k // per == b, 1.0, 0.0)
        pre[u, k] = part
        exchange(u, k, part)
        if u == 0 and k < CHUNKS - 1:
            send_wo(k + 1)
        if u == 0 and k == CHUNKS - 1:
            send(
                tg.at[:, :, p, :, target_cols(1 - b)], tgp.at[b], at["tg"], (far, c)
            )

    def hidden(u, k):
        v = pre[u, k] + exchanged(u, k)
        gate = jax.nn.sigmoid(v)
        hf[u, k] = (v * gate).astype(BF16)
        pre[u, k] = gate * (1.0 + v * (1.0 - gate))
        terms(u, k, hf[u, k], wo, plain, a)
        if u > 0:
            other_terms(u, k)

    def other_terms(u, k):
        if u == 0 and k == 0:
            for j in range(CHUNKS):
                part = pl.ds(j * (wo.shape[0] // CHUNKS), wo.shape[0] // CHUNKS)
                arrived(wox.at[part], at["wo"] + j)
        terms(u, k, hf[u, k], wox, plain, 1 - a)
        to_near("h", u, k, hf.at[u, k], hb)

    def next_state(u, k):
        new = (sf[u, k, q, p].astype(F32) + total(u, k)).astype(BF16)
        own[u, k] = new
        if u == 0:
            sf[1, k, q, p] = new
            spread(sf.at[1], "ag0", k)
            piece_to_near("s", 1, k, sf.at[1], sb)
        dots(u, k)

    def last_grad(u, k):
        dots_in(u, k)
        gf[1, k, q, p] = cosine(u, k).astype(BF16)
        spread(gf.at[1], "ag1", k)
        piece_to_near("g", 1, k, gf.at[1], gb)

    def into_back(u, k):
        collect(gf.at[u], f"ag{2 - u}", k)
        part = mm(flat(gf[u, k, a]), wo[...], flipped) + mm(
            flat(gf[u, k, 1 - a]), wox[...], flipped
        )
        back[k] = part
        exchange(3 - u, k, part)
        if u == 1:
            half_to_near("s", 0, k, sf, sb)

    def hidden_grad(u, k):
        ef[u, k] = ((back[k] + exchanged(3 - u, k)) * pre[u, k]).astype(BF16)
        if u > 0:
            terms(2, k, ef[u, k], wi, flipped, a)
            terms(2, k, ef[u, k], wix, flipped, 1 - a)
        to_near("e", u, k, ef.at[u, k], eb)

    def first_grad(u, k):
        half_to_twin("s", 0, k, sb)
        if k == 0:
            for j in range(CHUNKS):
                dots_in(0, j)
        summed = gf[1, k, q, p].astype(F32) + total(2, k) + cosine(0, k)
        gf[0, k, q, p] = summed.astype(BF16)
        spread(gf.at[0], "ag2", k)
        piece_to_near("g", 0, k, gf.at[0], gb)

    back = [None] * CHUNKS
    for o in (4, 2, 6):
        j = toggled(c, o)
        j = j + 1 - 2 * q
        arrived(place0(j), at["s0"] + j)
    arrived(place0(twin), at["s0"] + twin)
    for load in loads[:3]:
        load.wait()
    acts = [
        mm((act[u:u + 1] == ids).astype(F32).astype(BF16), emb[...], over_rows) for u in range(2)
    ]
    run = dict(
        into_hidden=into_hidden, hidden=hidden, other_terms=other_terms, next_state=next_state,
        last_grad=last_grad, into_back=into_back, hidden_grad=hidden_grad, first_grad=first_grad,
    )
    for name, u, k in stage_order():
        if name == "next_state" and u == 0 and k == 0:
            arrived(tgp.at[1 - b], at["tg"])
            loads[4].wait()
        if name == "hidden" and u == 0 and k == 0:
            loads[3].wait()
        run[name](u, k)
        if k == CHUNKS - 1:
            if name == "into_hidden" and u == 1:
                share("s", 1, sb)
            elif name == "into_back" and u == 1:
                complete("s", 1, sb)
                share("g", 1, gb)
            elif name == "into_back" and u == 0:
                complete("g", 1, gb)
                share("g", 0, gb)

    def out(acc, u, left, right, first):
        val = mm(left, right, over_rows)
        acc[...] = val if first else acc[...] + val

    def near_out(acc, u, left, right, first):
        out(acc, u, flat(left[u]), flat(right[u]), first)

    complete("g", 0, gb)
    from_near("h", hb, 1)
    from_near("h", hb, 0)
    out(gwo, 1, flat(hf[1]), flat(gf[1, :, a]), True)
    out(gwo, 0, flat(hf[0]), flat(gf[0, :, a]), False)
    completed("g", 1, gb)
    completed("g", 0, gb)
    near_out(gwo, 1, hb, gb, False)
    near_out(gwo, 0, hb, gb, False)
    gwo_store.start()
    completed("s", 1, sb)
    from_twin("s", sb, 0)
    from_near("e", eb, 1)
    out(gwi, 1, flat(sf[1, :, a]), flat(ef[1]), True)
    out(gwi, 0, flat(sf[0, :, a]), flat(ef[0]), False)
    near_out(gwi, 1, sb, eb, False)

    for src, dst, sem, slot, dev, when in started:
        if when is None:
            copy(src, dst, sem, slot, dev).wait_send()
        else:
            pl.when(when)(lambda: copy(src, dst, sem, slot, dev).wait_send())
    from_near("e", eb, 0)
    near_out(gwi, 0, sb, eb, False)
    gwi_store.start()
    gwo_store.wait()
    gwi_store.wait()


def paired(nc, state_start, actions, targets, w_in, w_out, action_embed):
    rb, sw = state_start.shape
    df, fc = w_in.shape
    groups = nc // 2
    per = CHUNKS // 2
    piece = rb // (per * groups)
    rows = groups * piece
    hbm = pl.BlockSpec(memory_space=pltpu.HBM)
    _, receives = sem_plan(nc)
    state = pltpu.VMEM((2, CHUNKS, 2, groups, piece, df), BF16)
    hid = pltpu.VMEM((2, CHUNKS, rows, fc), BF16)
    feat = pltpu.VMEM((2, CHUNKS, rows, df), BF16)
    return pl.pallas_call(
        kernel,
        out_shape=(
            jax.ShapeDtypeStruct((df, fc), F32),
            jax.ShapeDtypeStruct((fc, df), F32),
        ),
        in_specs=[hbm] * 6,
        out_specs=(hbm, hbm),
        scratch_shapes=[
            pltpu.VMEM((df, fc), BF16),
            pltpu.VMEM((fc, df), BF16),
            pltpu.VMEM((2, rb), jnp.int32),
            pltpu.VMEM(action_embed.shape, BF16),
            pltpu.VMEM((df, fc), F32),
            pltpu.VMEM((fc, df), F32),
            pltpu.VMEM((df, fc), BF16),
            pltpu.VMEM((fc, df), BF16),
            pltpu.VMEM((per, groups, piece, sw), BF16),
            pltpu.VMEM((2, 2, per, piece, df), BF16),
            state,
            state,
            hid,
            hid,
            pltpu.VMEM((2, CHUNKS, groups, piece, df), BF16),
            pltpu.VMEM((2, CHUNKS, groups, piece, df), BF16),
            hid,
            hid,
            pltpu.VMEM((4, CHUNKS, rows, fc), BF16),
            pltpu.VMEM((4, CHUNKS, rows, fc), BF16),
            pltpu.VMEM((3, CHUNKS, 2, groups, piece, df), BF16),
            pltpu.VMEM((3, CHUNKS, nc, piece, df), BF16),
            pltpu.VMEM((2, CHUNKS, piece, df), BF16),
            pltpu.VMEM((2, CHUNKS, rows, fc), F32),
            pltpu.VMEM((2, CHUNKS, piece, 128), F32),
            pltpu.VMEM((2, CHUNKS, 4, piece, 128), F32),
            pltpu.SemaphoreType.DMA((sends_in_all(nc),)),
            pltpu.SemaphoreType.DMA((receives,)),
            pltpu.SemaphoreType.DMA((8,)),
        ],
        compiler_params=pltpu.CompilerParams(
            collective_id=0, has_side_effects=True, vmem_limit_bytes=56 * 1024 * 1024
        ),
    )(
        state_start.reshape(per, groups, piece, sw),
        actions.T,
        targets.reshape(targets.shape[0], per, groups, piece, targets.shape[2]),
        w_in,
        w_out,
        action_embed,
    )


def solution(mesh):
    nr, nc = mesh.shape["row"], mesh.shape["col"]

    def on_device(state_start, actions, targets, w_in, w_out, action_embed):
        rb, sw = state_start.shape
        fits = (
            targets.shape[0] == 2
            and nr == 4
            and nc == 8
            and rb % (16 * (CHUNKS // 2) * (nc // 2)) == 0
            and sw % 128 == 0
            and w_in.shape[0] == 2 * sw
            and w_in.shape[1] % (128 * CHUNKS) == 0
        )
        args = (state_start, actions, targets, w_in, w_out, action_embed)
        if fits:
            return paired(nc, *args)
        return gathered(*args)

    in_specs = (
        P("row", "col"),
        P("row", None),
        P(None, "row", None),
        P("row", "col"),
        P("col", "row"),
        P(None, "col"),
    )
    out_specs = (P("row", "col"), P("col", "row"))
    return jax.shard_map(
        on_device, mesh=mesh, in_specs=in_specs, out_specs=out_specs, check_vma=False
    )
```

```python
import functools

import jax
import jax.numpy as jnp
from jax import lax
from jax.experimental import pallas as pl
from jax.experimental.pallas import tpu as pltpu
from jax.sharding import PartitionSpec as P

EPS = 1e-06
LOSS_SCALE = 128.0
MESH = pl.DeviceIdType.MESH
F32 = jnp.float32
BF16 = jnp.bfloat16


def silu_grad(pre_act):
    gate_val = jax.nn.sigmoid(pre_act)
    return gate_val * (1.0 + pre_act * (1.0 - gate_val))


def cosine_from(state_f, target_f, self_dot, cross_dot, target_dot):
    inv_state = lax.rsqrt(self_dot + EPS)
    inv_target = lax.rsqrt(target_dot + EPS)
    cosine = cross_dot * inv_state * inv_target
    return -LOSS_SCALE * (
        target_f * inv_state * inv_target - cosine * state_f * inv_state * inv_state
    )


def shared_cosine(state, target):
    state_f = state.astype(jnp.float32)
    target_f = target.astype(jnp.float32)
    self_dot, cross_dot, target_dot = lax.psum(
        (
            jnp.sum(state_f * state_f, axis=-1),
            jnp.sum(state_f * target_f, axis=-1),
            jnp.sum(target_f * target_f, axis=-1),
        ),
        "col",
    )
    return cosine_from(
        state_f, target_f, self_dot[:, None], cross_dot[:, None], target_dot[:, None]
    )


def gathered(state_start, actions, targets, w_in, w_out, action_embed):
    unroll_steps = targets.shape[0]
    col_width = state_start.shape[1]
    w_in_panel = lax.all_gather(w_in, "row", axis=0, tiled=True)
    w_out_panel = lax.all_gather(w_out, "row", axis=1, tiled=True)
    col_start = lax.axis_index("col") * col_width
    action_ids = jnp.arange(action_embed.shape[0], dtype=jnp.int32)
    contract_last = (((1,), (1,)), ((), ()))
    current = state_start
    full_states = []
    pre_list = []
    hidden_list = []
    cos_terms = []
    for unroll in range(unroll_steps):
        full_rows = lax.all_gather(current, "col", axis=1, tiled=True)
        onehot = (actions[:, unroll][:, None] == action_ids[None, :]).astype(jnp.bfloat16)
        pre_act = jnp.dot(full_rows, w_in_panel, preferred_element_type=jnp.float32) + jnp.dot(
            onehot, action_embed, preferred_element_type=jnp.float32
        )
        hidden = jax.nn.silu(pre_act).astype(jnp.bfloat16)
        partial_value = jnp.dot(hidden, w_out_panel, preferred_element_type=jnp.float32)
        target = targets[unroll]
        branch = lax.psum_scatter(
            partial_value.astype(jnp.bfloat16), "col", scatter_dimension=1, tiled=True
        ).astype(jnp.float32)
        current = (current.astype(jnp.float32) + branch).astype(jnp.bfloat16)
        target_slice = lax.dynamic_slice_in_dim(target, col_start, col_width, 1)
        cos_terms.append(shared_cosine(current, target_slice))
        full_states.append(full_rows)
        pre_list.append(pre_act)
        hidden_list.append(hidden)
    state_grad = cos_terms[unroll_steps - 1].astype(jnp.bfloat16)
    grad_list = [None] * unroll_steps
    hid_grads = [None] * unroll_steps
    for unroll in reversed(range(unroll_steps)):
        grad_rows = lax.all_gather(state_grad, "col", axis=1, tiled=True)
        back = lax.dot_general(
            grad_rows, w_out_panel, contract_last, preferred_element_type=jnp.float32
        )
        hid_grad = (back * silu_grad(pre_list[unroll])).astype(jnp.bfloat16)
        grad_list[unroll] = grad_rows
        hid_grads[unroll] = hid_grad
        if unroll > 0:
            input_part = lax.dot_general(
                hid_grad, w_in_panel, contract_last, preferred_element_type=jnp.float32
            )
            summed = lax.psum_scatter(
                input_part.astype(jnp.bfloat16), "col", scatter_dimension=1, tiled=True
            ).astype(jnp.float32)
            state_grad = (state_grad.astype(jnp.float32) + summed + cos_terms[unroll - 1]).astype(
                jnp.bfloat16
            )
    grad_stack = jnp.stack(grad_list)
    hidden_stack = jnp.stack(hidden_list)
    state_stack = jnp.stack(full_states)
    hid_stack = jnp.stack(hid_grads)
    grad_feature_blocks = lax.all_to_all(grad_stack, "row", split_axis=2, concat_axis=1, tiled=True)
    hidden_all = lax.all_gather(hidden_stack, "row", axis=1, tiled=True)
    grad_w_out = jnp.einsum(
        "kbf,kbd->fd", hidden_all, grad_feature_blocks, preferred_element_type=jnp.float32
    )
    state_feature_blocks = lax.all_to_all(
        state_stack, "row", split_axis=2, concat_axis=1, tiled=True
    )
    hid_all = lax.all_gather(hid_stack, "row", axis=1, tiled=True)
    grad_w_in = jnp.einsum(
        "kbd,kbf->df", state_feature_blocks, hid_all, preferred_element_type=jnp.float32
    )
    return (grad_w_in, grad_w_out)


CHUNKS = 4
STAGES = (
    ("into_hidden", 0, 0.0, 1.0),
    ("hidden", 0, 5.5, 2.4),
    ("other_terms", 0, 12.0, 1.0),
    ("next_state", 0, 16.0, 1.0),
    ("into_hidden", 1, 20.0, 1.0),
    ("hidden", 1, 25.5, 2.4),
    ("next_state", 1, 30.5, 2.4),
    ("last_grad", 1, 33.8, 2.4),
    ("into_back", 1, 38.0, 2.4),
    ("hidden_grad", 1, 43.5, 2.4),
    ("first_grad", 0, 48.0, 2.4),
    ("into_back", 0, 52.0, 2.4),
    ("hidden_grad", 0, 57.5, 2.4),
)


def stage_order():
    at = [
        (start + lag * k, i, k)
        for i, (_, _, start, lag) in enumerate(STAGES)
        for k in range(CHUNKS)
    ]
    return [(STAGES[i][0], STAGES[i][1], k) for _, i, k in sorted(at)]


def sem_plan(nc):
    at = {}
    total = 0
    for name, count in (
        [("wi", 1), ("wo", CHUNKS), ("s0x", 1), ("s0", nc), ("tg", 1)]
        + [(f"{n}t{u}", CHUNKS) for n in "sg" for u in range(2)]
        + [(f"{n}p{u}", 4) for n in "sg" for u in range(2)]
        + [(f"ag{i}", CHUNKS * nc) for i in range(3)]
        + [(f"z{i}", CHUNKS) for i in range(4)]
        + [(f"rs{i}", CHUNKS * nc) for i in range(3)]
        + [(f"dot{i}", CHUNKS * 4) for i in range(2)]
        + [(f"{n}b{u}", CHUNKS) for n in "hesg" for u in range(2)]
    ):
        at[name] = total
        total += count
    return at, total


def sends_in_all(nc):
    return 3 + CHUNKS + 2 * nc + CHUNKS * (6 * (nc - 1) + 3 + 4 + 6 + 8 + 4) + 12


def kernel(
    st, act_in, tg, wi_in, wo_in, emb_in, gwi_out, gwo_out,
    wi, wo, act, emb, gwi, gwo, wix, wox, s0x, tgp, sf, gf, hf, ef, sb, gb, hb, eb, zs, zr, ys, cr, own, pre, ds, dz,
    send_sem, recv_sem, load_sem,
):
    r, c = lax.axis_index("row"), lax.axis_index("col")
    nr, nc = 4, 8
    groups, piece, df = sf.shape[3], sf.shape[4], sf.shape[5]
    rows = groups * piece
    per = CHUNKS // 2
    sw = st.shape[3]
    a, b = lax.rem(r, 2), lax.div(r, 2)
    p, q = lax.div(c, 2), lax.rem(c, 2)
    near, far = r + 1 - 2 * a, lax.rem(r + 2, nr)
    twin = c + 1 - 2 * q
    at, _ = sem_plan(nc)
    started = []
    unused = iter(range(10000))

    def toggled(v, bits):
        for bit in (1, 2, 4):
            if bits & bit:
                v = v + bit - 2 * bit * lax.rem(lax.div(v, bit), 2)
        return v

    def cpeer(o):
        return toggled(c, (6, 7, 4, 5, 2, 3, 1)[o - 1])

    def copy(src, dst, sem, slot, dev):
        return pltpu.make_async_remote_copy(
            src_ref=src, dst_ref=dst, send_sem=send_sem.at[sem], recv_sem=recv_sem.at[slot],
            device_id=dev, device_id_type=MESH,
        )

    def send(src, dst, slot, dev, when=None):
        sem = next(unused)
        started.append((src, dst, sem, slot, dev, when))
        if when is None:
            copy(src, dst, sem, slot, dev).start()
        else:
            pl.when(when)(lambda: copy(src, dst, sem, slot, dev).start())

    def arrived(dst, slot, when=None):
        if when is None:
            copy(dst, dst, 0, slot, (near, c)).wait_recv()
        else:
            pl.when(when)(lambda: copy(dst, dst, 0, slot, (near, c)).wait_recv())

    home = lax.div(c, nc // 2) == b
    away = jnp.logical_not(home)

    def place0(col):
        i = jnp.where(lax.div(col, nc // 2) == b, b, 1 - b)
        return sf.at[
            0, pl.ds(i * per, per), lax.rem(lax.div(col, 2), 2), :, :,
            pl.ds(pl.multiple_of(lax.rem(col, 2) * sw, sw), sw),
        ]

    def target_cols(plane_half):
        return pl.ds(pl.multiple_of((2 * plane_half + q) * df, df), df)

    loads = [
        pltpu.make_async_copy(src, dst, load_sem.at[i])
        for i, (src, dst) in enumerate((
            (wi_in, wi), (act_in, act), (emb_in, emb), (wo_in, wo),
            (tg.at[:, :, p, :, target_cols(b)], tgp.at[b]),
        ))
    ]
    keep = pltpu.make_async_copy(st, place0(c), load_sem.at[5])
    for load in loads:
        load.start()
    pl.when(home)(lambda: keep.start())
    gwo_store = pltpu.make_async_copy(gwo, gwo_out, load_sem.at[6])
    gwi_stores = [
        pltpu.make_async_copy(
            gwi.at[pl.ds(j * (df // 2), df // 2)], gwi_out.at[pl.ds(j * (df // 2), df // 2)],
            load_sem.at[7 + j],
        )
        for j in range(2)
    ]

    barrier = pltpu.get_barrier_semaphore()
    greeted = [(r, cpeer(o)) for o in range(1, nc)] + [
        (near, c), (far, c), (far, twin), (far, toggled(c, 4))
    ]
    for dev in greeted:
        pl.semaphore_signal(barrier, inc=1, device_id=dev, device_id_type=MESH)
    pl.semaphore_wait(barrier, len(greeted))

    send(st, s0x, at["s0x"], (far, toggled(c, 4)), away)
    for o in (6, 4, 2):
        send(st, place0(c), at["s0"] + c, (r, toggled(c, o)), home)
    send(st, place0(c), at["s0"] + c, (r, twin), home)
    send(wi_in, wix, at["wi"], (near, c))

    def send_wo(j):
        part = pl.ds(j * (wo.shape[0] // CHUNKS), wo.shape[0] // CHUNKS)
        send(wo_in.at[part], wox.at[part], at["wo"] + j, (near, c))

    send_wo(0)
    arrived(s0x, at["s0x"], away)
    for o in (6, 4, 2):
        send(s0x, place0(c), at["s0"] + c, (r, toggled(c, o)), away)
    send(s0x, place0(c), at["s0"] + c, (r, twin), away)

    @pl.when(away)
    def _():
        place0(c)[...] = s0x[...]

    for o in (4, 2, 6):
        j = toggled(c, o)
        arrived(place0(j), at["s0"] + j)
        send(place0(j), place0(j), at["s0"] + j, (r, twin))
    pl.when(home)(lambda: keep.wait())

    def mm(x, y, dims):
        return lax.dot_general(x, y, (dims, ((), ())), preferred_element_type=F32)

    def flat(x):
        return x.reshape(-1, x.shape[-1])

    ids = lax.broadcasted_iota(jnp.int32, (emb.shape[0], per * rows), 0)
    plain, flipped, over_rows = ((1,), (0,)), ((1,), (1,)), ((0,), (0,))

    def spread(full, name, k):
        for o in range(1, nc):
            send(full.at[k, q, p], full.at[k, q, p], at[name] + k * nc + c, (r, cpeer(o)))

    def collect(full, name, k):
        for o in range(1, nc):
            j = cpeer(o)
            arrived(full.at[k, lax.rem(j, 2), lax.div(j, 2)], at[name] + k * nc + j)

    def exchange(phase, k, part):
        zs[phase, k] = part.astype(BF16)
        send(zs.at[phase, k], zr.at[phase, k], at[f"z{phase}"] + k, (far, c))

    def exchanged(phase, k):
        arrived(zr.at[phase, k], at[f"z{phase}"] + k)
        return zr[phase, k].astype(F32)

    def to_near(name, u, k, src, dst):
        send(src, dst.at[u, k], at[f"{name}b{u}"] + k, (near, c))

    mine = pl.ds(q * (groups // 2), groups // 2)
    others = pl.ds((1 - q) * (groups // 2), groups // 2)

    def half_to_near(name, u, k, src, dst):
        send(src.at[u, k, 1 - a, mine], dst.at[u, k, mine], at[f"{name}b{u}"] + k, (near, c))

    def half_to_twin(name, u, k, dst):
        arrived(dst.at[u, k, mine], at[f"{name}b{u}"] + k)
        send(dst.at[u, k, mine], dst.at[u, k, mine], at[f"{name}t{u}"] + k, (r, twin))

    def piece_to_near(name, u, k, src, dst):
        send(src.at[k, q, p], dst.at[u, k, p], at[f"{name}b{u}"] + k, (near, c), q != a)

    def share(name, u, dst):
        for k in range(CHUNKS):
            arrived(dst.at[u, k, p], at[f"{name}b{u}"] + k, q == a)
        for o in (6, 4, 2):
            send(dst.at[u, :, p], dst.at[u, :, p], at[f"{name}p{u}"] + p, (r, toggled(c, o)), q == a)

    def complete(name, u, dst):
        for o in (1, 2, 3):
            g = toggled(p, o)
            arrived(dst.at[u, :, g], at[f"{name}p{u}"] + g, q == a)
        send(dst.at[u], dst.at[u], at[f"{name}t{u}"], (r, twin), q == a)

    def completed(name, u, dst):
        arrived(dst.at[u], at[f"{name}t{u}"], q != a)

    def from_twin(name, dst, u):
        for k in range(CHUNKS):
            arrived(dst.at[u, k, others], at[f"{name}t{u}"] + k)

    def from_near(name, dst, u):
        for k in range(CHUNKS):
            arrived(dst.at[u, k], at[f"{name}b{u}"] + k)

    def terms(phase, k, left, weight, dims, which):
        ys[phase, k, which] = mm(left, weight[...], dims).astype(BF16).reshape(groups, piece, df)
        for o in range(groups - 1, -1, -1):
            g = toggled(p, o)
            send(
                ys.at[phase, k, which, g], cr.at[phase, k, c], at[f"rs{phase}"] + k * nc + c,
                (r, 2 * g + which), which != q if o == 0 else None,
            )

    def total(phase, k):
        out = ys[phase, k, q, p].astype(F32)
        for o in range(1, nc):
            j = cpeer(o)
            arrived(cr.at[phase, k, j], at[f"rs{phase}"] + k * nc + j)
            out = out + cr[phase, k, j].astype(F32)
        return out

    lane = lax.broadcasted_iota(jnp.int32, (piece, 128), 1)

    def target(u, k):
        return tgp[k // per, u, k % per].astype(F32)

    def dots(u, k):
        s = own[u, k].astype(F32)
        t = target(u, k)
        ss = jnp.sum(s * s, axis=-1, keepdims=True)
        sc = jnp.sum(s * t, axis=-1, keepdims=True)
        tt = jnp.sum(t * t, axis=-1, keepdims=True)
        both = jnp.where(lane == 0, ss, jnp.where(lane == 1, sc, tt))
        me = 2 * b + q
        ds[u, k] = both
        dz[u, k, me] = both
        for dev in ((far, c), (far, twin), (r, twin)):
            send(ds.at[u, k], dz.at[u, k, me], at[f"dot{u}"] + k * 4 + me, dev)

    def dots_in(u, k):
        for o in range(1, 4):
            j = lax.rem(2 * b + q + o, 4)
            arrived(dz.at[u, k, j], at[f"dot{u}"] + k * 4 + j)

    def cosine(u, k):
        both = dz[u, k, 0]
        for j in range(1, 4):
            both = both + dz[u, k, j]
        return cosine_from(
            own[u, k].astype(F32), target(u, k), both[:, 0:1], both[:, 1:2], both[:, 2:3]
        )

    def into_hidden(u, k):
        if u > 0:
            collect(sf.at[u], "ag0", k)
        part = mm(flat(sf[u, k, a]), wi[...], plain)
        if u == 0 and k == 0:
            arrived(wix, at["wi"])
        part = part + mm(flat(sf[u, k, 1 - a]), wix[...], plain)
        part = part + acts[u][rows * (k % per):rows * (k % per) + rows] * jnp.where(k // per == b, 1.0, 0.0)
        pre[u, k] = part
        exchange(u, k, part)
        if u == 1:
            half_to_near("s", 0, k, sf, sb)
        if u == 0 and k < CHUNKS - 1:
            send_wo(k + 1)
        if u == 0 and k == CHUNKS - 1:
            send(
                tg.at[:, :, p, :, target_cols(1 - b)], tgp.at[b], at["tg"], (far, c)
            )

    def hidden(u, k):
        v = pre[u, k] + exchanged(u, k)
        gate = jax.nn.sigmoid(v)
        hf[u, k] = (v * gate).astype(BF16)
        pre[u, k] = gate * (1.0 + v * (1.0 - gate))
        terms(u, k, hf[u, k], wo, plain, a)
        if u > 0:
            other_terms(u, k)

    def other_terms(u, k):
        if u == 0 and k == 0:
            for j in range(CHUNKS):
                part = pl.ds(j * (wo.shape[0] // CHUNKS), wo.shape[0] // CHUNKS)
                arrived(wox.at[part], at["wo"] + j)
        terms(u, k, hf[u, k], wox, plain, 1 - a)
        to_near("h", u, k, hf.at[u, k], hb)

    def next_state(u, k):
        new = (sf[u, k, q, p].astype(F32) + total(u, k)).astype(BF16)
        own[u, k] = new
        if u == 0:
            sf[1, k, q, p] = new
            spread(sf.at[1], "ag0", k)
            piece_to_near("s", 1, k, sf.at[1], sb)
        dots(u, k)

    def last_grad(u, k):
        dots_in(u, k)
        gf[1, k, q, p] = cosine(u, k).astype(BF16)
        spread(gf.at[1], "ag1", k)
        piece_to_near("g", 1, k, gf.at[1], gb)

    def into_back(u, k):
        collect(gf.at[u], f"ag{2 - u}", k)
        part = mm(flat(gf[u, k, a]), wo[...], flipped) + mm(
            flat(gf[u, k, 1 - a]), wox[...], flipped
        )
        back[k] = part
        exchange(3 - u, k, part)

    def hidden_grad(u, k):
        ef[u, k] = ((back[k] + exchanged(3 - u, k)) * pre[u, k]).astype(BF16)
        if u > 0:
            terms(2, k, ef[u, k], wi, flipped, a)
            terms(2, k, ef[u, k], wix, flipped, 1 - a)
        to_near("e", u, k, ef.at[u, k], eb)

    def first_grad(u, k):
        half_to_twin("s", 0, k, sb)
        if k == 0:
            for j in range(CHUNKS):
                dots_in(0, j)
        summed = gf[1, k, q, p].astype(F32) + total(2, k) + cosine(0, k)
        gf[0, k, q, p] = summed.astype(BF16)
        spread(gf.at[0], "ag2", k)
        piece_to_near("g", 0, k, gf.at[0], gb)

    back = [None] * CHUNKS
    for o in (4, 2, 6):
        j = toggled(c, o)
        j = j + 1 - 2 * q
        arrived(place0(j), at["s0"] + j)
    arrived(place0(twin), at["s0"] + twin)
    for load in loads[:3]:
        load.wait()
    acts = [
        mm((act[u:u + 1] == ids).astype(F32).astype(BF16), emb[...], over_rows) for u in range(2)
    ]
    run = dict(
        into_hidden=into_hidden, hidden=hidden, other_terms=other_terms, next_state=next_state,
        last_grad=last_grad, into_back=into_back, hidden_grad=hidden_grad, first_grad=first_grad,
    )
    for name, u, k in stage_order():
        if name == "next_state" and u == 0 and k == 0:
            arrived(tgp.at[1 - b], at["tg"])
            loads[4].wait()
        if name == "hidden" and u == 0 and k == 0:
            loads[3].wait()
        run[name](u, k)
        if k == CHUNKS - 1:
            if name == "into_hidden" and u == 1:
                share("s", 1, sb)
            elif name == "into_back" and u == 1:
                complete("s", 1, sb)
                share("g", 1, gb)
            elif name == "into_back" and u == 0:
                complete("g", 1, gb)
                share("g", 0, gb)

    def out(acc, u, left, right, first):
        val = mm(left, right, over_rows)
        acc[...] = val if first else acc[...] + val

    def near_out(acc, u, left, right, first):
        out(acc, u, flat(left[u]), flat(right[u]), first)

    complete("g", 0, gb)
    from_near("h", hb, 1)
    from_near("h", hb, 0)
    out(gwo, 1, flat(hf[1]), flat(gf[1, :, a]), True)
    out(gwo, 0, flat(hf[0]), flat(gf[0, :, a]), False)
    completed("g", 1, gb)
    completed("g", 0, gb)
    near_out(gwo, 1, hb, gb, False)
    near_out(gwo, 0, hb, gb, False)
    gwo_store.start()
    completed("s", 1, sb)
    from_twin("s", sb, 0)
    from_near("e", eb, 1)
    out(gwi, 1, flat(sf[1, :, a]), flat(ef[1]), True)
    out(gwi, 0, flat(sf[0, :, a]), flat(ef[0]), False)
    near_out(gwi, 1, sb, eb, False)

    for src, dst, sem, slot, dev, when in started:
        if when is None:
            copy(src, dst, sem, slot, dev).wait_send()
        else:
            pl.when(when)(lambda: copy(src, dst, sem, slot, dev).wait_send())
    for k in range(CHUNKS - 1):
        arrived(eb.at[0, k], at["eb0"] + k)
    out(gwi, 0, flat(sb[0, :CHUNKS - 1]), flat(eb[0, :CHUNKS - 1]), False)
    arrived(eb.at[0, CHUNKS - 1], at["eb0"] + CHUNKS - 1)
    last = flat(sb[0, CHUNKS - 1])
    for j in range(2):
        part = slice(j * (df // 2), (j + 1) * (df // 2))
        gwi[part] += mm(last[:, part], eb[0, CHUNKS - 1], over_rows)
        gwi_stores[j].start()
    gwo_store.wait()
    for j in range(2):
        gwi_stores[j].wait()


def paired(nc, state_start, actions, targets, w_in, w_out, action_embed):
    rb, sw = state_start.shape
    df, fc = w_in.shape
    groups = nc // 2
    per = CHUNKS // 2
    piece = rb // (per * groups)
    rows = groups * piece
    hbm = pl.BlockSpec(memory_space=pltpu.HBM)
    _, receives = sem_plan(nc)
    state = pltpu.VMEM((2, CHUNKS, 2, groups, piece, df), BF16)
    hid = pltpu.VMEM((2, CHUNKS, rows, fc), BF16)
    feat = pltpu.VMEM((2, CHUNKS, rows, df), BF16)
    return pl.pallas_call(
        kernel,
        out_shape=(
            jax.ShapeDtypeStruct((df, fc), F32),
            jax.ShapeDtypeStruct((fc, df), F32),
        ),
        in_specs=[hbm] * 6,
        out_specs=(hbm, hbm),
        scratch_shapes=[
            pltpu.VMEM((df, fc), BF16),
            pltpu.VMEM((fc, df), BF16),
            pltpu.VMEM((2, rb), jnp.int32),
            pltpu.VMEM(action_embed.shape, BF16),
            pltpu.VMEM((df, fc), F32),
            pltpu.VMEM((fc, df), F32),
            pltpu.VMEM((df, fc), BF16),
            pltpu.VMEM((fc, df), BF16),
            pltpu.VMEM((per, groups, piece, sw), BF16),
            pltpu.VMEM((2, 2, per, piece, df), BF16),
            state,
            state,
            hid,
            hid,
            pltpu.VMEM((2, CHUNKS, groups, piece, df), BF16),
            pltpu.VMEM((2, CHUNKS, groups, piece, df), BF16),
            hid,
            hid,
            pltpu.VMEM((4, CHUNKS, rows, fc), BF16),
            pltpu.VMEM((4, CHUNKS, rows, fc), BF16),
            pltpu.VMEM((3, CHUNKS, 2, groups, piece, df), BF16),
            pltpu.VMEM((3, CHUNKS, nc, piece, df), BF16),
            pltpu.VMEM((2, CHUNKS, piece, df), BF16),
            pltpu.VMEM((2, CHUNKS, rows, fc), F32),
            pltpu.VMEM((2, CHUNKS, piece, 128), F32),
            pltpu.VMEM((2, CHUNKS, 4, piece, 128), F32),
            pltpu.SemaphoreType.DMA((sends_in_all(nc),)),
            pltpu.SemaphoreType.DMA((receives,)),
            pltpu.SemaphoreType.DMA((9,)),
        ],
        compiler_params=pltpu.CompilerParams(
            collective_id=0, has_side_effects=True, vmem_limit_bytes=56 * 1024 * 1024
        ),
    )(
        state_start.reshape(per, groups, piece, sw),
        actions.T,
        targets.reshape(targets.shape[0], per, groups, piece, targets.shape[2]),
        w_in,
        w_out,
        action_embed,
    )


def solution(mesh):
    nr, nc = mesh.shape["row"], mesh.shape["col"]

    def on_device(state_start, actions, targets, w_in, w_out, action_embed):
        rb, sw = state_start.shape
        fits = (
            targets.shape[0] == 2
            and nr == 4
            and nc == 8
            and rb % (16 * (CHUNKS // 2) * (nc // 2)) == 0
            and sw % 128 == 0
            and w_in.shape[0] == 2 * sw
            and w_in.shape[1] % (128 * CHUNKS) == 0
        )
        args = (state_start, actions, targets, w_in, w_out, action_embed)
        if fits:
            return paired(nc, *args)
        return gathered(*args)

    in_specs = (
        P("row", "col"),
        P("row", None),
        P(None, "row", None),
        P("row", "col"),
        P("col", "row"),
        P(None, "col"),
    )
    out_specs = (P("row", "col"), P("col", "row"))
    return jax.shard_map(
        on_device, mesh=mesh, in_specs=in_specs, out_specs=out_specs, check_vma=False
    )
```

```python
import functools

import jax
import jax.numpy as jnp
from jax import lax
from jax.experimental import pallas as pl
from jax.experimental.pallas import tpu as pltpu
from jax.sharding import PartitionSpec as P

EPS = 1e-06
LOSS_SCALE = 128.0
MESH = pl.DeviceIdType.MESH
F32 = jnp.float32
BF16 = jnp.bfloat16


def silu_grad(pre_act):
    gate_val = jax.nn.sigmoid(pre_act)
    return gate_val * (1.0 + pre_act * (1.0 - gate_val))


def cosine_from(state_f, target_f, self_dot, cross_dot, target_dot):
    inv_state = lax.rsqrt(self_dot + EPS)
    inv_target = lax.rsqrt(target_dot + EPS)
    cosine = cross_dot * inv_state * inv_target
    return -LOSS_SCALE * (
        target_f * inv_state * inv_target - cosine * state_f * inv_state * inv_state
    )


def shared_cosine(state, target):
    state_f = state.astype(jnp.float32)
    target_f = target.astype(jnp.float32)
    self_dot, cross_dot, target_dot = lax.psum(
        (
            jnp.sum(state_f * state_f, axis=-1),
            jnp.sum(state_f * target_f, axis=-1),
            jnp.sum(target_f * target_f, axis=-1),
        ),
        "col",
    )
    return cosine_from(
        state_f, target_f, self_dot[:, None], cross_dot[:, None], target_dot[:, None]
    )


def gathered(state_start, actions, targets, w_in, w_out, action_embed):
    unroll_steps = targets.shape[0]
    col_width = state_start.shape[1]
    w_in_panel = lax.all_gather(w_in, "row", axis=0, tiled=True)
    w_out_panel = lax.all_gather(w_out, "row", axis=1, tiled=True)
    col_start = lax.axis_index("col") * col_width
    action_ids = jnp.arange(action_embed.shape[0], dtype=jnp.int32)
    contract_last = (((1,), (1,)), ((), ()))
    current = state_start
    full_states = []
    pre_list = []
    hidden_list = []
    cos_terms = []
    for unroll in range(unroll_steps):
        full_rows = lax.all_gather(current, "col", axis=1, tiled=True)
        onehot = (actions[:, unroll][:, None] == action_ids[None, :]).astype(jnp.bfloat16)
        pre_act = jnp.dot(full_rows, w_in_panel, preferred_element_type=jnp.float32) + jnp.dot(
            onehot, action_embed, preferred_element_type=jnp.float32
        )
        hidden = jax.nn.silu(pre_act).astype(jnp.bfloat16)
        partial_value = jnp.dot(hidden, w_out_panel, preferred_element_type=jnp.float32)
        target = targets[unroll]
        branch = lax.psum_scatter(
            partial_value.astype(jnp.bfloat16), "col", scatter_dimension=1, tiled=True
        ).astype(jnp.float32)
        current = (current.astype(jnp.float32) + branch).astype(jnp.bfloat16)
        target_slice = lax.dynamic_slice_in_dim(target, col_start, col_width, 1)
        cos_terms.append(shared_cosine(current, target_slice))
        full_states.append(full_rows)
        pre_list.append(pre_act)
        hidden_list.append(hidden)
    state_grad = cos_terms[unroll_steps - 1].astype(jnp.bfloat16)
    grad_list = [None] * unroll_steps
    hid_grads = [None] * unroll_steps
    for unroll in reversed(range(unroll_steps)):
        grad_rows = lax.all_gather(state_grad, "col", axis=1, tiled=True)
        back = lax.dot_general(
            grad_rows, w_out_panel, contract_last, preferred_element_type=jnp.float32
        )
        hid_grad = (back * silu_grad(pre_list[unroll])).astype(jnp.bfloat16)
        grad_list[unroll] = grad_rows
        hid_grads[unroll] = hid_grad
        if unroll > 0:
            input_part = lax.dot_general(
                hid_grad, w_in_panel, contract_last, preferred_element_type=jnp.float32
            )
            summed = lax.psum_scatter(
                input_part.astype(jnp.bfloat16), "col", scatter_dimension=1, tiled=True
            ).astype(jnp.float32)
            state_grad = (state_grad.astype(jnp.float32) + summed + cos_terms[unroll - 1]).astype(
                jnp.bfloat16
            )
    grad_stack = jnp.stack(grad_list)
    hidden_stack = jnp.stack(hidden_list)
    state_stack = jnp.stack(full_states)
    hid_stack = jnp.stack(hid_grads)
    grad_feature_blocks = lax.all_to_all(grad_stack, "row", split_axis=2, concat_axis=1, tiled=True)
    hidden_all = lax.all_gather(hidden_stack, "row", axis=1, tiled=True)
    grad_w_out = jnp.einsum(
        "kbf,kbd->fd", hidden_all, grad_feature_blocks, preferred_element_type=jnp.float32
    )
    state_feature_blocks = lax.all_to_all(
        state_stack, "row", split_axis=2, concat_axis=1, tiled=True
    )
    hid_all = lax.all_gather(hid_stack, "row", axis=1, tiled=True)
    grad_w_in = jnp.einsum(
        "kbd,kbf->df", state_feature_blocks, hid_all, preferred_element_type=jnp.float32
    )
    return (grad_w_in, grad_w_out)


CHUNKS = 4
STAGES = (
    ("into_hidden", 0, 0.0, 1.0),
    ("hidden", 0, 5.5, 2.4),
    ("other_terms", 0, 12.0, 1.0),
    ("next_state", 0, 16.0, 1.0),
    ("into_hidden", 1, 20.0, 1.0),
    ("hidden", 1, 25.5, 2.4),
    ("next_state", 1, 30.5, 2.4),
    ("last_grad", 1, 33.8, 2.4),
    ("into_back", 1, 38.0, 2.4),
    ("hidden_grad", 1, 43.5, 2.4),
    ("first_grad", 0, 48.0, 2.4),
    ("into_back", 0, 52.0, 2.4),
    ("hidden_grad", 0, 57.5, 2.4),
)


def stage_order():
    at = [
        (start + lag * k, i, k)
        for i, (_, _, start, lag) in enumerate(STAGES)
        for k in range(CHUNKS)
    ]
    return [(STAGES[i][0], STAGES[i][1], k) for _, i, k in sorted(at)]


def sem_plan(nc):
    at = {}
    total = 0
    for name, count in (
        [("wi", 1), ("wo", CHUNKS), ("s0x", 1), ("s0", nc), ("tg", 1)]
        + [(f"{n}t{u}", CHUNKS) for n in "sg" for u in range(2)]
        + [(f"{n}p{u}", 4) for n in "sg" for u in range(2)]
        + [(f"ag{i}", CHUNKS * nc) for i in range(3)]
        + [(f"z{i}", CHUNKS) for i in range(4)]
        + [(f"rs{i}", CHUNKS * nc) for i in range(3)]
        + [(f"dot{i}", CHUNKS * 4) for i in range(2)]
        + [(f"{n}b{u}", CHUNKS) for n in "hesg" for u in range(2)]
    ):
        at[name] = total
        total += count
    return at, total


def sends_in_all(nc):
    return 3 + CHUNKS + 2 * nc + CHUNKS * (6 * (nc - 1) + 3 + 4 + 6 + 8 + 4) + 12


def kernel(
    st, act_in, tg, wi_in, wo_in, emb_in, gwi_out, gwo_out,
    wi, wo, act, emb, gwi, gwo, wix, wox, s0x, tgp, sf, gf, hf, ef, sb, gb, hb, eb, zs, zr, ys, cr, own, pre, ds, dz,
    send_sem, recv_sem, load_sem,
):
    r, c = lax.axis_index("row"), lax.axis_index("col")
    nr, nc = 4, 8
    groups, piece, df = sf.shape[3], sf.shape[4], sf.shape[5]
    rows = groups * piece
    per = CHUNKS // 2
    sw = st.shape[3]
    a, b = lax.rem(r, 2), lax.div(r, 2)
    p, q = lax.div(c, 2), lax.rem(c, 2)
    near, far = r + 1 - 2 * a, lax.rem(r + 2, nr)
    twin = c + 1 - 2 * q
    at, _ = sem_plan(nc)
    started = []
    unused = iter(range(10000))

    def toggled(v, bits):
        for bit in (1, 2, 4):
            if bits & bit:
                v = v + bit - 2 * bit * lax.rem(lax.div(v, bit), 2)
        return v

    def cpeer(o):
        return toggled(c, (6, 7, 4, 5, 2, 3, 1)[o - 1])

    def copy(src, dst, sem, slot, dev):
        return pltpu.make_async_remote_copy(
            src_ref=src, dst_ref=dst, send_sem=send_sem.at[sem], recv_sem=recv_sem.at[slot],
            device_id=dev, device_id_type=MESH,
        )

    def send(src, dst, slot, dev, when=None):
        sem = next(unused)
        started.append((src, dst, sem, slot, dev, when))
        if when is None:
            copy(src, dst, sem, slot, dev).start()
        else:
            pl.when(when)(lambda: copy(src, dst, sem, slot, dev).start())

    def arrived(dst, slot, when=None):
        if when is None:
            copy(dst, dst, 0, slot, (near, c)).wait_recv()
        else:
            pl.when(when)(lambda: copy(dst, dst, 0, slot, (near, c)).wait_recv())

    home = lax.div(c, nc // 2) == b
    away = jnp.logical_not(home)

    def place0(col):
        i = jnp.where(lax.div(col, nc // 2) == b, b, 1 - b)
        return sf.at[
            0, pl.ds(i * per, per), lax.rem(lax.div(col, 2), 2), :, :,
            pl.ds(pl.multiple_of(lax.rem(col, 2) * sw, sw), sw),
        ]

    def target_cols(plane_half):
        return pl.ds(pl.multiple_of((2 * plane_half + q) * df, df), df)

    barrier = pltpu.get_barrier_semaphore()
    greeted = [(r, cpeer(o)) for o in range(1, nc)] + [
        (near, c), (far, c), (far, twin), (far, toggled(c, 4))
    ]
    for dev in greeted:
        pl.semaphore_signal(barrier, inc=1, device_id=dev, device_id_type=MESH)
    loads = [
        pltpu.make_async_copy(src, dst, load_sem.at[i])
        for i, (src, dst) in enumerate((
            (wi_in, wi), (act_in, act), (emb_in, emb), (wo_in, wo),
            (tg.at[:, :, p, :, target_cols(b)], tgp.at[b]),
        ))
    ]
    keep = pltpu.make_async_copy(st, place0(c), load_sem.at[5])
    for load in loads:
        load.start()
    pl.when(home)(lambda: keep.start())
    gwo_store = pltpu.make_async_copy(gwo, gwo_out, load_sem.at[6])
    gwi_stores = [
        pltpu.make_async_copy(
            gwi.at[pl.ds(j * (df // 2), df // 2)], gwi_out.at[pl.ds(j * (df // 2), df // 2)],
            load_sem.at[7 + j],
        )
        for j in range(2)
    ]

    pl.semaphore_wait(barrier, len(greeted))

    send(st, s0x, at["s0x"], (far, toggled(c, 4)), away)
    for o in (6, 4, 2):
        send(st, place0(c), at["s0"] + c, (r, toggled(c, o)), home)
    send(st, place0(c), at["s0"] + c, (r, twin), home)
    send(wi_in, wix, at["wi"], (near, c))

    def send_wo(j):
        part = pl.ds(j * (wo.shape[0] // CHUNKS), wo.shape[0] // CHUNKS)
        send(wo_in.at[part], wox.at[part], at["wo"] + j, (near, c))

    send_wo(0)
    arrived(s0x, at["s0x"], away)
    for o in (6, 4, 2):
        send(s0x, place0(c), at["s0"] + c, (r, toggled(c, o)), away)
    send(s0x, place0(c), at["s0"] + c, (r, twin), away)

    @pl.when(away)
    def _():
        place0(c)[...] = s0x[...]

    for o in (4, 2, 6):
        j = toggled(c, o)
        arrived(place0(j), at["s0"] + j)
        send(place0(j), place0(j), at["s0"] + j, (r, twin))
    pl.when(home)(lambda: keep.wait())

    def mm(x, y, dims):
        return lax.dot_general(x, y, (dims, ((), ())), preferred_element_type=F32)

    def flat(x):
        return x.reshape(-1, x.shape[-1])

    ids = lax.broadcasted_iota(jnp.int32, (emb.shape[0], per * rows), 0)
    plain, flipped, over_rows = ((1,), (0,)), ((1,), (1,)), ((0,), (0,))

    def spread(full, name, k):
        for o in range(1, nc):
            send(full.at[k, q, p], full.at[k, q, p], at[name] + k * nc + c, (r, cpeer(o)))

    def collect(full, name, k):
        for o in range(1, nc):
            j = cpeer(o)
            arrived(full.at[k, lax.rem(j, 2), lax.div(j, 2)], at[name] + k * nc + j)

    def exchange(phase, k, part):
        zs[phase, k] = part.astype(BF16)
        send(zs.at[phase, k], zr.at[phase, k], at[f"z{phase}"] + k, (far, c))

    def exchanged(phase, k):
        arrived(zr.at[phase, k], at[f"z{phase}"] + k)
        return zr[phase, k].astype(F32)

    def to_near(name, u, k, src, dst):
        send(src, dst.at[u, k], at[f"{name}b{u}"] + k, (near, c))

    mine = pl.ds(q * (groups // 2), groups // 2)
    others = pl.ds((1 - q) * (groups // 2), groups // 2)

    def half_to_near(name, u, k, src, dst):
        send(src.at[u, k, 1 - a, mine], dst.at[u, k, mine], at[f"{name}b{u}"] + k, (near, c))

    def half_to_twin(name, u, k, dst):
        arrived(dst.at[u, k, mine], at[f"{name}b{u}"] + k)
        send(dst.at[u, k, mine], dst.at[u, k, mine], at[f"{name}t{u}"] + k, (r, twin))

    def piece_to_near(name, u, k, src, dst):
        send(src.at[k, q, p], dst.at[u, k, p], at[f"{name}b{u}"] + k, (near, c), q != a)

    def share(name, u, dst):
        for k in range(CHUNKS):
            arrived(dst.at[u, k, p], at[f"{name}b{u}"] + k, q == a)
        for o in (6, 4, 2):
            send(dst.at[u, :, p], dst.at[u, :, p], at[f"{name}p{u}"] + p, (r, toggled(c, o)), q == a)

    def complete(name, u, dst):
        for o in (1, 2, 3):
            g = toggled(p, o)
            arrived(dst.at[u, :, g], at[f"{name}p{u}"] + g, q == a)
        send(dst.at[u], dst.at[u], at[f"{name}t{u}"], (r, twin), q == a)

    def completed(name, u, dst):
        arrived(dst.at[u], at[f"{name}t{u}"], q != a)

    def from_twin(name, dst, u):
        for k in range(CHUNKS):
            arrived(dst.at[u, k, others], at[f"{name}t{u}"] + k)

    def from_near(name, dst, u):
        for k in range(CHUNKS):
            arrived(dst.at[u, k], at[f"{name}b{u}"] + k)

    def terms(phase, k, left, weight, dims, which):
        ys[phase, k, which] = mm(left, weight[...], dims).astype(BF16).reshape(groups, piece, df)
        for o in range(groups - 1, -1, -1):
            g = toggled(p, o)
            send(
                ys.at[phase, k, which, g], cr.at[phase, k, c], at[f"rs{phase}"] + k * nc + c,
                (r, 2 * g + which), which != q if o == 0 else None,
            )

    def total(phase, k):
        out = ys[phase, k, q, p].astype(F32)
        for o in range(1, nc):
            j = cpeer(o)
            arrived(cr.at[phase, k, j], at[f"rs{phase}"] + k * nc + j)
            out = out + cr[phase, k, j].astype(F32)
        return out

    lane = lax.broadcasted_iota(jnp.int32, (piece, 128), 1)

    def target(u, k):
        return tgp[k // per, u, k % per].astype(F32)

    def dots(u, k):
        s = own[u, k].astype(F32)
        t = target(u, k)
        ss = jnp.sum(s * s, axis=-1, keepdims=True)
        sc = jnp.sum(s * t, axis=-1, keepdims=True)
        tt = jnp.sum(t * t, axis=-1, keepdims=True)
        both = jnp.where(lane == 0, ss, jnp.where(lane == 1, sc, tt))
        me = 2 * b + q
        ds[u, k] = both
        dz[u, k, me] = both
        for dev in ((far, c), (far, twin), (r, twin)):
            send(ds.at[u, k], dz.at[u, k, me], at[f"dot{u}"] + k * 4 + me, dev)

    def dots_in(u, k):
        for o in range(1, 4):
            j = lax.rem(2 * b + q + o, 4)
            arrived(dz.at[u, k, j], at[f"dot{u}"] + k * 4 + j)

    def cosine(u, k):
        both = dz[u, k, 0]
        for j in range(1, 4):
            both = both + dz[u, k, j]
        return cosine_from(
            own[u, k].astype(F32), target(u, k), both[:, 0:1], both[:, 1:2], both[:, 2:3]
        )

    def into_hidden(u, k):
        if u > 0:
            collect(sf.at[u], "ag0", k)
        part = mm(flat(sf[u, k, a]), wi[...], plain)
        if u == 0 and k == 0:
            arrived(wix, at["wi"])
        part = part + mm(flat(sf[u, k, 1 - a]), wix[...], plain)
        part = part + acts[u][rows * (k % per):rows * (k % per) + rows] * jnp.where(k // per == b, 1.0, 0.0)
        pre[u, k] = part
        exchange(u, k, part)
        if u == 1:
            half_to_near("s", 0, k, sf, sb)
        if u == 0 and k < CHUNKS - 1:
            send_wo(k + 1)
        if u == 0 and k == CHUNKS - 1:
            send(
                tg.at[:, :, p, :, target_cols(1 - b)], tgp.at[b], at["tg"], (far, c)
            )

    def hidden(u, k):
        v = pre[u, k] + exchanged(u, k)
        gate = jax.nn.sigmoid(v)
        hf[u, k] = (v * gate).astype(BF16)
        pre[u, k] = gate * (1.0 + v * (1.0 - gate))
        terms(u, k, hf[u, k], wo, plain, a)
        if u > 0:
            other_terms(u, k)

    def other_terms(u, k):
        if u == 0 and k == 0:
            for j in range(CHUNKS):
                part = pl.ds(j * (wo.shape[0] // CHUNKS), wo.shape[0] // CHUNKS)
                arrived(wox.at[part], at["wo"] + j)
        terms(u, k, hf[u, k], wox, plain, 1 - a)
        to_near("h", u, k, hf.at[u, k], hb)

    def next_state(u, k):
        new = (sf[u, k, q, p].astype(F32) + total(u, k)).astype(BF16)
        own[u, k] = new
        if u == 0:
            sf[1, k, q, p] = new
            spread(sf.at[1], "ag0", k)
            piece_to_near("s", 1, k, sf.at[1], sb)
        dots(u, k)

    def last_grad(u, k):
        dots_in(u, k)
        gf[1, k, q, p] = cosine(u, k).astype(BF16)
        spread(gf.at[1], "ag1", k)
        piece_to_near("g", 1, k, gf.at[1], gb)

    def into_back(u, k):
        collect(gf.at[u], f"ag{2 - u}", k)
        part = mm(flat(gf[u, k, a]), wo[...], flipped) + mm(
            flat(gf[u, k, 1 - a]), wox[...], flipped
        )
        back[k] = part
        exchange(3 - u, k, part)

    def hidden_grad(u, k):
        ef[u, k] = ((back[k] + exchanged(3 - u, k)) * pre[u, k]).astype(BF16)
        if u > 0:
            terms(2, k, ef[u, k], wi, flipped, a)
            terms(2, k, ef[u, k], wix, flipped, 1 - a)
        to_near("e", u, k, ef.at[u, k], eb)

    def first_grad(u, k):
        half_to_twin("s", 0, k, sb)
        if k == 0:
            for j in range(CHUNKS):
                dots_in(0, j)
        summed = gf[1, k, q, p].astype(F32) + total(2, k) + cosine(0, k)
        gf[0, k, q, p] = summed.astype(BF16)
        spread(gf.at[0], "ag2", k)
        piece_to_near("g", 0, k, gf.at[0], gb)

    back = [None] * CHUNKS
    for o in (4, 2, 6):
        j = toggled(c, o)
        j = j + 1 - 2 * q
        arrived(place0(j), at["s0"] + j)
    arrived(place0(twin), at["s0"] + twin)
    for load in loads[:3]:
        load.wait()
    acts = [
        mm((act[u:u + 1] == ids).astype(F32).astype(BF16), emb[...], over_rows) for u in range(2)
    ]
    run = dict(
        into_hidden=into_hidden, hidden=hidden, other_terms=other_terms, next_state=next_state,
        last_grad=last_grad, into_back=into_back, hidden_grad=hidden_grad, first_grad=first_grad,
    )
    for name, u, k in stage_order():
        if name == "next_state" and u == 0 and k == 0:
            arrived(tgp.at[1 - b], at["tg"])
            loads[4].wait()
        if name == "hidden" and u == 0 and k == 0:
            loads[3].wait()
        run[name](u, k)
        if k == CHUNKS - 1:
            if name == "into_hidden" and u == 1:
                share("s", 1, sb)
            elif name == "into_back" and u == 1:
                complete("s", 1, sb)
                share("g", 1, gb)
            elif name == "into_back" and u == 0:
                complete("g", 1, gb)
                share("g", 0, gb)

    def out(acc, u, left, right, first):
        val = mm(left, right, over_rows)
        acc[...] = val if first else acc[...] + val

    def near_out(acc, u, left, right, first):
        out(acc, u, flat(left[u]), flat(right[u]), first)

    complete("g", 0, gb)
    from_near("h", hb, 1)
    from_near("h", hb, 0)
    out(gwo, 1, flat(hf[1]), flat(gf[1, :, a]), True)
    out(gwo, 0, flat(hf[0]), flat(gf[0, :, a]), False)
    completed("g", 1, gb)
    completed("g", 0, gb)
    near_out(gwo, 1, hb, gb, False)
    near_out(gwo, 0, hb, gb, False)
    gwo_store.start()
    completed("s", 1, sb)
    from_twin("s", sb, 0)
    from_near("e", eb, 1)
    out(gwi, 1, flat(sf[1, :, a]), flat(ef[1]), True)
    out(gwi, 0, flat(sf[0, :, a]), flat(ef[0]), False)
    near_out(gwi, 1, sb, eb, False)

    for src, dst, sem, slot, dev, when in started:
        if when is None:
            copy(src, dst, sem, slot, dev).wait_send()
        else:
            pl.when(when)(lambda: copy(src, dst, sem, slot, dev).wait_send())
    for k in range(CHUNKS - 1):
        arrived(eb.at[0, k], at["eb0"] + k)
    out(gwi, 0, flat(sb[0, :CHUNKS - 1]), flat(eb[0, :CHUNKS - 1]), False)
    arrived(eb.at[0, CHUNKS - 1], at["eb0"] + CHUNKS - 1)
    last = flat(sb[0, CHUNKS - 1])
    for j in range(2):
        part = slice(j * (df // 2), (j + 1) * (df // 2))
        gwi[part] += mm(last[:, part], eb[0, CHUNKS - 1], over_rows)
        gwi_stores[j].start()
    gwo_store.wait()
    for j in range(2):
        gwi_stores[j].wait()


def paired(nc, state_start, actions, targets, w_in, w_out, action_embed):
    rb, sw = state_start.shape
    df, fc = w_in.shape
    groups = nc // 2
    per = CHUNKS // 2
    piece = rb // (per * groups)
    rows = groups * piece
    hbm = pl.BlockSpec(memory_space=pltpu.HBM)
    _, receives = sem_plan(nc)
    state = pltpu.VMEM((2, CHUNKS, 2, groups, piece, df), BF16)
    hid = pltpu.VMEM((2, CHUNKS, rows, fc), BF16)
    feat = pltpu.VMEM((2, CHUNKS, rows, df), BF16)
    return pl.pallas_call(
        kernel,
        out_shape=(
            jax.ShapeDtypeStruct((df, fc), F32),
            jax.ShapeDtypeStruct((fc, df), F32),
        ),
        in_specs=[hbm] * 6,
        out_specs=(hbm, hbm),
        scratch_shapes=[
            pltpu.VMEM((df, fc), BF16),
            pltpu.VMEM((fc, df), BF16),
            pltpu.VMEM((2, rb), jnp.int32),
            pltpu.VMEM(action_embed.shape, BF16),
            pltpu.VMEM((df, fc), F32),
            pltpu.VMEM((fc, df), F32),
            pltpu.VMEM((df, fc), BF16),
            pltpu.VMEM((fc, df), BF16),
            pltpu.VMEM((per, groups, piece, sw), BF16),
            pltpu.VMEM((2, 2, per, piece, df), BF16),
            state,
            state,
            hid,
            hid,
            pltpu.VMEM((2, CHUNKS, groups, piece, df), BF16),
            pltpu.VMEM((2, CHUNKS, groups, piece, df), BF16),
            hid,
            hid,
            pltpu.VMEM((4, CHUNKS, rows, fc), BF16),
            pltpu.VMEM((4, CHUNKS, rows, fc), BF16),
            pltpu.VMEM((3, CHUNKS, 2, groups, piece, df), BF16),
            pltpu.VMEM((3, CHUNKS, nc, piece, df), BF16),
            pltpu.VMEM((2, CHUNKS, piece, df), BF16),
            pltpu.VMEM((2, CHUNKS, rows, fc), F32),
            pltpu.VMEM((2, CHUNKS, piece, 128), F32),
            pltpu.VMEM((2, CHUNKS, 4, piece, 128), F32),
            pltpu.SemaphoreType.DMA((sends_in_all(nc),)),
            pltpu.SemaphoreType.DMA((receives,)),
            pltpu.SemaphoreType.DMA((9,)),
        ],
        compiler_params=pltpu.CompilerParams(
            collective_id=0, has_side_effects=True, vmem_limit_bytes=56 * 1024 * 1024
        ),
    )(
        state_start.reshape(per, groups, piece, sw),
        actions.T,
        targets.reshape(targets.shape[0], per, groups, piece, targets.shape[2]),
        w_in,
        w_out,
        action_embed,
    )


def solution(mesh):
    nr, nc = mesh.shape["row"], mesh.shape["col"]

    def on_device(state_start, actions, targets, w_in, w_out, action_embed):
        rb, sw = state_start.shape
        fits = (
            targets.shape[0] == 2
            and nr == 4
            and nc == 8
            and rb % (16 * (CHUNKS // 2) * (nc // 2)) == 0
            and sw % 128 == 0
            and w_in.shape[0] == 2 * sw
            and w_in.shape[1] % (128 * CHUNKS) == 0
        )
        args = (state_start, actions, targets, w_in, w_out, action_embed)
        if fits:
            return paired(nc, *args)
        return gathered(*args)

    in_specs = (
        P("row", "col"),
        P("row", None),
        P(None, "row", None),
        P("row", "col"),
        P("col", "row"),
        P(None, "col"),
    )
    out_specs = (P("row", "col"), P("col", "row"))
    return jax.shard_map(
        on_device, mesh=mesh, in_specs=in_specs, out_specs=out_specs, check_vma=False
    )
```

```python
import functools

import jax
import jax.numpy as jnp
from jax import lax
from jax.experimental import pallas as pl
from jax.experimental.pallas import tpu as pltpu
from jax.sharding import PartitionSpec as P

EPS = 1e-06
LOSS_SCALE = 128.0
MESH = pl.DeviceIdType.MESH
F32 = jnp.float32
BF16 = jnp.bfloat16


def silu_grad(pre_act):
    gate_val = jax.nn.sigmoid(pre_act)
    return gate_val * (1.0 + pre_act * (1.0 - gate_val))


def cosine_from(state_f, target_f, self_dot, cross_dot, target_dot):
    inv_state = lax.rsqrt(self_dot + EPS)
    inv_target = lax.rsqrt(target_dot + EPS)
    cosine = cross_dot * inv_state * inv_target
    return -LOSS_SCALE * (
        target_f * inv_state * inv_target - cosine * state_f * inv_state * inv_state
    )


def shared_cosine(state, target):
    state_f = state.astype(jnp.float32)
    target_f = target.astype(jnp.float32)
    self_dot, cross_dot, target_dot = lax.psum(
        (
            jnp.sum(state_f * state_f, axis=-1),
            jnp.sum(state_f * target_f, axis=-1),
            jnp.sum(target_f * target_f, axis=-1),
        ),
        "col",
    )
    return cosine_from(
        state_f, target_f, self_dot[:, None], cross_dot[:, None], target_dot[:, None]
    )


def gathered(state_start, actions, targets, w_in, w_out, action_embed):
    unroll_steps = targets.shape[0]
    col_width = state_start.shape[1]
    w_in_panel = lax.all_gather(w_in, "row", axis=0, tiled=True)
    w_out_panel = lax.all_gather(w_out, "row", axis=1, tiled=True)
    col_start = lax.axis_index("col") * col_width
    action_ids = jnp.arange(action_embed.shape[0], dtype=jnp.int32)
    contract_last = (((1,), (1,)), ((), ()))
    current = state_start
    full_states = []
    pre_list = []
    hidden_list = []
    cos_terms = []
    for unroll in range(unroll_steps):
        full_rows = lax.all_gather(current, "col", axis=1, tiled=True)
        onehot = (actions[:, unroll][:, None] == action_ids[None, :]).astype(jnp.bfloat16)
        pre_act = jnp.dot(full_rows, w_in_panel, preferred_element_type=jnp.float32) + jnp.dot(
            onehot, action_embed, preferred_element_type=jnp.float32
        )
        hidden = jax.nn.silu(pre_act).astype(jnp.bfloat16)
        partial_value = jnp.dot(hidden, w_out_panel, preferred_element_type=jnp.float32)
        target = targets[unroll]
        branch = lax.psum_scatter(
            partial_value.astype(jnp.bfloat16), "col", scatter_dimension=1, tiled=True
        ).astype(jnp.float32)
        current = (current.astype(jnp.float32) + branch).astype(jnp.bfloat16)
        target_slice = lax.dynamic_slice_in_dim(target, col_start, col_width, 1)
        cos_terms.append(shared_cosine(current, target_slice))
        full_states.append(full_rows)
        pre_list.append(pre_act)
        hidden_list.append(hidden)
    state_grad = cos_terms[unroll_steps - 1].astype(jnp.bfloat16)
    grad_list = [None] * unroll_steps
    hid_grads = [None] * unroll_steps
    for unroll in reversed(range(unroll_steps)):
        grad_rows = lax.all_gather(state_grad, "col", axis=1, tiled=True)
        back = lax.dot_general(
            grad_rows, w_out_panel, contract_last, preferred_element_type=jnp.float32
        )
        hid_grad = (back * silu_grad(pre_list[unroll])).astype(jnp.bfloat16)
        grad_list[unroll] = grad_rows
        hid_grads[unroll] = hid_grad
        if unroll > 0:
            input_part = lax.dot_general(
                hid_grad, w_in_panel, contract_last, preferred_element_type=jnp.float32
            )
            summed = lax.psum_scatter(
                input_part.astype(jnp.bfloat16), "col", scatter_dimension=1, tiled=True
            ).astype(jnp.float32)
            state_grad = (state_grad.astype(jnp.float32) + summed + cos_terms[unroll - 1]).astype(
                jnp.bfloat16
            )
    grad_stack = jnp.stack(grad_list)
    hidden_stack = jnp.stack(hidden_list)
    state_stack = jnp.stack(full_states)
    hid_stack = jnp.stack(hid_grads)
    grad_feature_blocks = lax.all_to_all(grad_stack, "row", split_axis=2, concat_axis=1, tiled=True)
    hidden_all = lax.all_gather(hidden_stack, "row", axis=1, tiled=True)
    grad_w_out = jnp.einsum(
        "kbf,kbd->fd", hidden_all, grad_feature_blocks, preferred_element_type=jnp.float32
    )
    state_feature_blocks = lax.all_to_all(
        state_stack, "row", split_axis=2, concat_axis=1, tiled=True
    )
    hid_all = lax.all_gather(hid_stack, "row", axis=1, tiled=True)
    grad_w_in = jnp.einsum(
        "kbd,kbf->df", state_feature_blocks, hid_all, preferred_element_type=jnp.float32
    )
    return (grad_w_in, grad_w_out)


CHUNKS = 4
STAGES = (
    ("into_hidden", 0, 0.0, 1.0),
    ("hidden", 0, 5.5, 2.4),
    ("other_terms", 0, 12.0, 1.0),
    ("next_state", 0, 16.0, 1.0),
    ("into_hidden", 1, 20.0, 1.0),
    ("hidden", 1, 25.5, 2.4),
    ("next_state", 1, 30.5, 2.4),
    ("last_grad", 1, 33.8, 2.4),
    ("into_back", 1, 38.0, 2.4),
    ("hidden_grad", 1, 43.5, 2.4),
    ("first_grad", 0, 48.0, 2.4),
    ("into_back", 0, 52.0, 2.4),
    ("hidden_grad", 0, 57.5, 2.4),
)


def stage_order():
    at = [
        (start + lag * k, i, k)
        for i, (_, _, start, lag) in enumerate(STAGES)
        for k in range(CHUNKS)
    ]
    return [(STAGES[i][0], STAGES[i][1], k) for _, i, k in sorted(at)]


def sem_plan(nc):
    at = {}
    total = 0
    for name, count in (
        [("wi", 1), ("wo", CHUNKS), ("s0x", 1), ("s0", nc), ("tg", 1)]
        + [(f"{n}t{u}", CHUNKS) for n in "sg" for u in range(2)]
        + [(f"{n}p{u}", 4) for n in "sg" for u in range(2)]
        + [(f"ag{i}", CHUNKS * nc) for i in range(3)]
        + [(f"z{i}", CHUNKS) for i in range(4)]
        + [(f"rs{i}", CHUNKS * nc) for i in range(3)]
        + [(f"dot{i}", CHUNKS * 4) for i in range(2)]
        + [(f"{n}b{u}", CHUNKS) for n in "hesg" for u in range(2)]
    ):
        at[name] = total
        total += count
    return at, total


def sends_in_all(nc):
    return 3 + CHUNKS + 2 * nc + CHUNKS * (6 * (nc - 1) + 3 + 4 + 6 + 8 + 4) + 12


def kernel(
    st, act_in, tg, wi_in, wo_in, emb_in, gwi_out, gwo_out,
    wi, wo, act, emb, gwi, gwo, wix, wox, s0x, tgp, sf, gf, hf, ef, sb, gb, hb, eb, zs, zr, ys, cr, own, pre, ds, dz,
    send_sem, recv_sem, load_sem,
):
    r, c = lax.axis_index("row"), lax.axis_index("col")
    nr, nc = 4, 8
    groups, piece, df = sf.shape[3], sf.shape[4], sf.shape[5]
    rows = groups * piece
    per = CHUNKS // 2
    sw = st.shape[3]
    a, b = lax.rem(r, 2), lax.div(r, 2)
    p, q = lax.div(c, 2), lax.rem(c, 2)
    near, far = r + 1 - 2 * a, lax.rem(r + 2, nr)
    twin = c + 1 - 2 * q
    at, _ = sem_plan(nc)
    started = []
    unused = iter(range(10000))

    def toggled(v, bits):
        for bit in (1, 2, 4):
            if bits & bit:
                v = v + bit - 2 * bit * lax.rem(lax.div(v, bit), 2)
        return v

    def cpeer(o):
        return toggled(c, (6, 7, 4, 5, 2, 3, 1)[o - 1])

    def copy(src, dst, sem, slot, dev):
        return pltpu.make_async_remote_copy(
            src_ref=src, dst_ref=dst, send_sem=send_sem.at[sem], recv_sem=recv_sem.at[slot],
            device_id=dev, device_id_type=MESH,
        )

    def send(src, dst, slot, dev, when=None):
        sem = next(unused)
        started.append((src, dst, sem, slot, dev, when))
        if when is None:
            copy(src, dst, sem, slot, dev).start()
        else:
            pl.when(when)(lambda: copy(src, dst, sem, slot, dev).start())

    def arrived(dst, slot, when=None):
        if when is None:
            copy(dst, dst, 0, slot, (near, c)).wait_recv()
        else:
            pl.when(when)(lambda: copy(dst, dst, 0, slot, (near, c)).wait_recv())

    home = lax.div(c, nc // 2) == b
    away = jnp.logical_not(home)

    def place0(col):
        i = jnp.where(lax.div(col, nc // 2) == b, b, 1 - b)
        return sf.at[
            0, pl.ds(i * per, per), lax.rem(lax.div(col, 2), 2), :, :,
            pl.ds(pl.multiple_of(lax.rem(col, 2) * sw, sw), sw),
        ]

    def target_cols(plane_half):
        return pl.ds(pl.multiple_of((2 * plane_half + q) * df, df), df)

    loads = [
        pltpu.make_async_copy(src, dst, load_sem.at[i])
        for i, (src, dst) in enumerate((
            (wi_in, wi), (act_in, act), (emb_in, emb), (wo_in, wo),
            (tg.at[:, :, p, :, target_cols(b)], tgp.at[b]),
        ))
    ]
    keep = pltpu.make_async_copy(st, place0(c), load_sem.at[5])
    for load in loads:
        load.start()
    pl.when(home)(lambda: keep.start())
    gwo_store = pltpu.make_async_copy(gwo, gwo_out, load_sem.at[6])
    gwi_store = pltpu.make_async_copy(gwi, gwi_out, load_sem.at[7])

    barrier = pltpu.get_barrier_semaphore()
    greeted = [(r, cpeer(o)) for o in range(1, nc)] + [
        (near, c), (far, c), (far, twin), (far, toggled(c, 4))
    ]
    for dev in greeted:
        pl.semaphore_signal(barrier, inc=1, device_id=dev, device_id_type=MESH)
    pl.semaphore_wait(barrier, len(greeted))

    send(st, s0x, at["s0x"], (far, toggled(c, 4)), away)
    for o in (6, 4, 2):
        send(st, place0(c), at["s0"] + c, (r, toggled(c, o)), home)
    send(st, place0(c), at["s0"] + c, (r, twin), home)
    send(wi_in, wix, at["wi"], (near, c))

    def send_wo(j):
        part = pl.ds(j * (wo.shape[0] // CHUNKS), wo.shape[0] // CHUNKS)
        send(wo_in.at[part], wox.at[part], at["wo"] + j, (near, c))

    send_wo(0)
    arrived(s0x, at["s0x"], away)
    for o in (6, 4, 2):
        send(s0x, place0(c), at["s0"] + c, (r, toggled(c, o)), away)
    send(s0x, place0(c), at["s0"] + c, (r, twin), away)

    @pl.when(away)
    def _():
        place0(c)[...] = s0x[...]

    for o in (4, 2, 6):
        j = toggled(c, o)
        arrived(place0(j), at["s0"] + j)
        send(place0(j), place0(j), at["s0"] + j, (r, twin))
    pl.when(home)(lambda: keep.wait())

    def mm(x, y, dims):
        return lax.dot_general(x, y, (dims, ((), ())), preferred_element_type=F32)

    def flat(x):
        return x.reshape(-1, x.shape[-1])

    ids = lax.broadcasted_iota(jnp.int32, (emb.shape[0], per * rows), 0)
    plain, flipped, over_rows = ((1,), (0,)), ((1,), (1,)), ((0,), (0,))

    def spread(full, name, k):
        for o in range(1, nc):
            send(full.at[k, q, p], full.at[k, q, p], at[name] + k * nc + c, (r, cpeer(o)))

    def collect(full, name, k):
        for o in range(1, nc):
            j = cpeer(o)
            arrived(full.at[k, lax.rem(j, 2), lax.div(j, 2)], at[name] + k * nc + j)

    def exchange(phase, k, part):
        zs[phase, k] = part.astype(BF16)
        send(zs.at[phase, k], zr.at[phase, k], at[f"z{phase}"] + k, (far, c))

    def exchanged(phase, k):
        arrived(zr.at[phase, k], at[f"z{phase}"] + k)
        return zr[phase, k].astype(F32)

    def to_near(name, u, k, src, dst):
        send(src, dst.at[u, k], at[f"{name}b{u}"] + k, (near, c))

    mine = pl.ds(q * (groups // 2), groups // 2)
    others = pl.ds((1 - q) * (groups // 2), groups // 2)

    def half_to_near(name, u, k, src, dst):
        send(src.at[u, k, 1 - a, mine], dst.at[u, k, mine], at[f"{name}b{u}"] + k, (near, c))

    def half_to_twin(name, u, k, dst):
        arrived(dst.at[u, k, mine], at[f"{name}b{u}"] + k)
        send(dst.at[u, k, mine], dst.at[u, k, mine], at[f"{name}t{u}"] + k, (r, twin))

    def piece_to_near(name, u, k, src, dst):
        send(src.at[k, q, p], dst.at[u, k, p], at[f"{name}b{u}"] + k, (near, c), q != a)

    def share(name, u, dst):
        for k in range(CHUNKS):
            arrived(dst.at[u, k, p], at[f"{name}b{u}"] + k, q == a)
        for o in (6, 4, 2):
            send(dst.at[u, :, p], dst.at[u, :, p], at[f"{name}p{u}"] + p, (r, toggled(c, o)), q == a)

    def complete(name, u, dst):
        for o in (1, 2, 3):
            g = toggled(p, o)
            arrived(dst.at[u, :, g], at[f"{name}p{u}"] + g, q == a)
        send(dst.at[u], dst.at[u], at[f"{name}t{u}"], (r, twin), q == a)

    def completed(name, u, dst):
        arrived(dst.at[u], at[f"{name}t{u}"], q != a)

    def from_twin(name, dst, u):
        for k in range(CHUNKS):
            arrived(dst.at[u, k, others], at[f"{name}t{u}"] + k)

    def from_near(name, dst, u):
        for k in range(CHUNKS):
            arrived(dst.at[u, k], at[f"{name}b{u}"] + k)

    def terms(phase, k, left, weight, dims, which):
        ys[phase, k, which] = mm(left, weight[...], dims).astype(BF16).reshape(groups, piece, df)
        for o in range(groups - 1, -1, -1):
            g = toggled(p, o)
            send(
                ys.at[phase, k, which, g], cr.at[phase, k, c], at[f"rs{phase}"] + k * nc + c,
                (r, 2 * g + which), which != q if o == 0 else None,
            )

    def total(phase, k):
        out = ys[phase, k, q, p].astype(F32)
        for o in range(1, nc):
            j = cpeer(o)
            arrived(cr.at[phase, k, j], at[f"rs{phase}"] + k * nc + j)
            out = out + cr[phase, k, j].astype(F32)
        return out

    lane = lax.broadcasted_iota(jnp.int32, (piece, 128), 1)

    def target(u, k):
        return tgp[k // per, u, k % per].astype(F32)

    def dots(u, k):
        s = own[u, k].astype(F32)
        t = target(u, k)
        ss = jnp.sum(s * s, axis=-1, keepdims=True)
        sc = jnp.sum(s * t, axis=-1, keepdims=True)
        tt = jnp.sum(t * t, axis=-1, keepdims=True)
        both = jnp.where(lane == 0, ss, jnp.where(lane == 1, sc, tt))
        me = 2 * b + q
        ds[u, k] = both
        dz[u, k, me] = both
        for dev in ((far, c), (far, twin), (r, twin)):
            send(ds.at[u, k], dz.at[u, k, me], at[f"dot{u}"] + k * 4 + me, dev)

    def dots_in(u, k):
        for o in range(1, 4):
            j = lax.rem(2 * b + q + o, 4)
            arrived(dz.at[u, k, j], at[f"dot{u}"] + k * 4 + j)

    def cosine(u, k):
        both = dz[u, k, 0]
        for j in range(1, 4):
            both = both + dz[u, k, j]
        return cosine_from(
            own[u, k].astype(F32), target(u, k), both[:, 0:1], both[:, 1:2], both[:, 2:3]
        )

    def into_hidden(u, k):
        if u > 0:
            collect(sf.at[u], "ag0", k)
        part = mm(flat(sf[u, k, a]), wi[...], plain)
        if u == 0 and k == 0:
            arrived(wix, at["wi"])
        part = part + mm(flat(sf[u, k, 1 - a]), wix[...], plain)
        part = part + acts[u][rows * (k % per):rows * (k % per) + rows] * jnp.where(k // per == b, 1.0, 0.0)
        pre[u, k] = part
        exchange(u, k, part)
        if u == 1:
            half_to_near("s", 0, k, sf, sb)
        if u == 0 and k < CHUNKS - 1:
            send_wo(k + 1)
        if u == 0 and k == CHUNKS - 1:
            send(
                tg.at[:, :, p, :, target_cols(1 - b)], tgp.at[b], at["tg"], (far, c)
            )

    def hidden(u, k):
        v = pre[u, k] + exchanged(u, k)
        gate = jax.nn.sigmoid(v)
        hf[u, k] = (v * gate).astype(BF16)
        pre[u, k] = gate * (1.0 + v * (1.0 - gate))
        terms(u, k, hf[u, k], wo, plain, a)
        if u > 0:
            other_terms(u, k)

    def other_terms(u, k):
        if u == 0 and k == 0:
            for j in range(CHUNKS):
                part = pl.ds(j * (wo.shape[0] // CHUNKS), wo.shape[0] // CHUNKS)
                arrived(wox.at[part], at["wo"] + j)
        terms(u, k, hf[u, k], wox, plain, 1 - a)
        to_near("h", u, k, hf.at[u, k], hb)

    def next_state(u, k):
        new = (sf[u, k, q, p].astype(F32) + total(u, k)).astype(BF16)
        own[u, k] = new
        if u == 0:
            sf[1, k, q, p] = new
            spread(sf.at[1], "ag0", k)
            piece_to_near("s", 1, k, sf.at[1], sb)
        dots(u, k)

    def last_grad(u, k):
        dots_in(u, k)
        gf[1, k, q, p] = cosine(u, k).astype(BF16)
        spread(gf.at[1], "ag1", k)
        piece_to_near("g", 1, k, gf.at[1], gb)

    def into_back(u, k):
        collect(gf.at[u], f"ag{2 - u}", k)
        part = mm(flat(gf[u, k, a]), wo[...], flipped) + mm(
            flat(gf[u, k, 1 - a]), wox[...], flipped
        )
        back[k] = part
        exchange(3 - u, k, part)

    def hidden_grad(u, k):
        ef[u, k] = ((back[k] + exchanged(3 - u, k)) * pre[u, k]).astype(BF16)
        if u > 0:
            terms(2, k, ef[u, k], wi, flipped, a)
            terms(2, k, ef[u, k], wix, flipped, 1 - a)
        to_near("e", u, k, ef.at[u, k], eb)

    def first_grad(u, k):
        half_to_twin("s", 0, k, sb)
        if k == 0:
            for j in range(CHUNKS):
                dots_in(0, j)
        summed = gf[1, k, q, p].astype(F32) + total(2, k) + cosine(0, k)
        gf[0, k, q, p] = summed.astype(BF16)
        spread(gf.at[0], "ag2", k)
        piece_to_near("g", 0, k, gf.at[0], gb)

    back = [None] * CHUNKS
    for o in (4, 2, 6):
        j = toggled(c, o)
        j = j + 1 - 2 * q
        arrived(place0(j), at["s0"] + j)
    arrived(place0(twin), at["s0"] + twin)
    for load in loads[:3]:
        load.wait()
    acts = [
        mm((act[u:u + 1] == ids).astype(F32).astype(BF16), emb[...], over_rows) for u in range(2)
    ]
    run = dict(
        into_hidden=into_hidden, hidden=hidden, other_terms=other_terms, next_state=next_state,
        last_grad=last_grad, into_back=into_back, hidden_grad=hidden_grad, first_grad=first_grad,
    )
    for name, u, k in stage_order():
        if name == "next_state" and u == 0 and k == 0:
            arrived(tgp.at[1 - b], at["tg"])
            loads[4].wait()
        if name == "hidden" and u == 0 and k == 0:
            loads[3].wait()
        run[name](u, k)
        if k == CHUNKS - 1:
            if name == "into_hidden" and u == 1:
                share("s", 1, sb)
            elif name == "into_back" and u == 1:
                complete("s", 1, sb)
                share("g", 1, gb)
            elif name == "into_back" and u == 0:
                complete("g", 1, gb)
                share("g", 0, gb)

    def out(acc, u, left, right, first):
        val = mm(left, right, over_rows)
        acc[...] = val if first else acc[...] + val

    def near_out(acc, u, left, right, first):
        out(acc, u, flat(left[u]), flat(right[u]), first)

    complete("g", 0, gb)
    from_near("h", hb, 1)
    from_near("h", hb, 0)
    out(gwo, 1, flat(hf[1]), flat(gf[1, :, a]), True)
    out(gwo, 0, flat(hf[0]), flat(gf[0, :, a]), False)
    completed("g", 1, gb)
    completed("g", 0, gb)
    near_out(gwo, 1, hb, gb, False)
    near_out(gwo, 0, hb, gb, False)
    gwo_store.start()
    completed("s", 1, sb)
    from_twin("s", sb, 0)
    from_near("e", eb, 1)
    out(gwi, 1, flat(sf[1, :, a]), flat(ef[1]), True)
    out(gwi, 0, flat(sf[0, :, a]), flat(ef[0]), False)
    near_out(gwi, 1, sb, eb, False)

    for src, dst, sem, slot, dev, when in started:
        if when is None:
            copy(src, dst, sem, slot, dev).wait_send()
        else:
            pl.when(when)(lambda: copy(src, dst, sem, slot, dev).wait_send())
    from_near("e", eb, 0)
    near_out(gwi, 0, sb, eb, False)
    gwi_store.start()
    gwo_store.wait()
    gwi_store.wait()


def paired(nc, state_start, actions, targets, w_in, w_out, action_embed):
    rb, sw = state_start.shape
    df, fc = w_in.shape
    groups = nc // 2
    per = CHUNKS // 2
    piece = rb // (per * groups)
    rows = groups * piece
    hbm = pl.BlockSpec(memory_space=pltpu.HBM)
    _, receives = sem_plan(nc)
    state = pltpu.VMEM((2, CHUNKS, 2, groups, piece, df), BF16)
    hid = pltpu.VMEM((2, CHUNKS, rows, fc), BF16)
    feat = pltpu.VMEM((2, CHUNKS, rows, df), BF16)
    return pl.pallas_call(
        kernel,
        out_shape=(
            jax.ShapeDtypeStruct((df, fc), F32),
            jax.ShapeDtypeStruct((fc, df), F32),
        ),
        in_specs=[hbm] * 6,
        out_specs=(hbm, hbm),
        scratch_shapes=[
            pltpu.VMEM((df, fc), BF16),
            pltpu.VMEM((fc, df), BF16),
            pltpu.VMEM((2, rb), jnp.int32),
            pltpu.VMEM(action_embed.shape, BF16),
            pltpu.VMEM((df, fc), F32),
            pltpu.VMEM((fc, df), F32),
            pltpu.VMEM((df, fc), BF16),
            pltpu.VMEM((fc, df), BF16),
            pltpu.VMEM((per, groups, piece, sw), BF16),
            pltpu.VMEM((2, 2, per, piece, df), BF16),
            state,
            state,
            hid,
            hid,
            pltpu.VMEM((2, CHUNKS, groups, piece, df), BF16),
            pltpu.VMEM((2, CHUNKS, groups, piece, df), BF16),
            hid,
            hid,
            pltpu.VMEM((4, CHUNKS, rows, fc), BF16),
            pltpu.VMEM((4, CHUNKS, rows, fc), BF16),
            pltpu.VMEM((3, CHUNKS, 2, groups, piece, df), BF16),
            pltpu.VMEM((3, CHUNKS, nc, piece, df), BF16),
            pltpu.VMEM((2, CHUNKS, piece, df), BF16),
            pltpu.VMEM((2, CHUNKS, rows, fc), F32),
            pltpu.VMEM((2, CHUNKS, piece, 128), F32),
            pltpu.VMEM((2, CHUNKS, 4, piece, 128), F32),
            pltpu.SemaphoreType.DMA((sends_in_all(nc),)),
            pltpu.SemaphoreType.DMA((receives,)),
            pltpu.SemaphoreType.DMA((8,)),
        ],
        compiler_params=pltpu.CompilerParams(
            collective_id=0, has_side_effects=True, vmem_limit_bytes=56 * 1024 * 1024
        ),
    )(
        state_start.reshape(per, groups, piece, sw),
        actions.T,
        targets.reshape(targets.shape[0], per, groups, piece, targets.shape[2]),
        w_in,
        w_out,
        action_embed,
    )


def solution(mesh):
    nr, nc = mesh.shape["row"], mesh.shape["col"]

    def on_device(state_start, actions, targets, w_in, w_out, action_embed):
        rb, sw = state_start.shape
        fits = (
            targets.shape[0] == 2
            and nr == 4
            and nc == 8
            and rb % (16 * (CHUNKS // 2) * (nc // 2)) == 0
            and sw % 128 == 0
            and w_in.shape[0] == 2 * sw
            and w_in.shape[1] % (128 * CHUNKS) == 0
        )
        args = (state_start, actions, targets, w_in, w_out, action_embed)
        if fits:
            return paired(nc, *args)
        return gathered(*args)

    in_specs = (
        P("row", "col"),
        P("row", None),
        P(None, "row", None),
        P("row", "col"),
        P("col", "row"),
        P(None, "col"),
    )
    out_specs = (P("row", "col"), P("col", "row"))
    return jax.shard_map(
        on_device, mesh=mesh, in_specs=in_specs, out_specs=out_specs, check_vma=False
    )
```
